128 devices in a mesh: seq: 8 (over x, core), exp: 16 (over y, z).
Axes of the slice: x: 4, y: 4, z: 4, core: 2. Of those that a mesh axis runs over, the one named last changes fastest.
Arguments:
- queries: bfloat16 [16, 512, 4096], P('exp', 'seq'), may hold values from -130 to 130
- new_keys: bfloat16 [16, 512, 512], P('exp', 'seq'), may hold values from -6 to 6
- new_values: bfloat16 [16, 512, 512], P('exp', 'seq'), may hold values from -6 to 6
- cache_keys: bfloat16 [16, 4096, 512], P('exp', 'seq'), may hold values from -7 to 7
- cache_values: bfloat16 [16, 4096, 512], P('exp', 'seq'), may hold values from -6 to 6
- cache_len: int32 [16], P('exp'), may hold values from 1024 to 4096, as said below
- residual_in: bfloat16 [16, 512, 2048], P('exp', 'seq'), may hold values from -6 to 6
- out_weight: bfloat16 [4096, 2048], P('seq'), may hold values from -0.09375 to 0.09375
- norm_gain: float32 [2048], replicated, may hold values from 0.25 to 1.75
- router_weight: bfloat16 [2048, 128], replicated, may hold values from -0.125 to 0.125
- expert_ids: int32 [16, 512, 8], P('exp', 'seq'), may hold values from 0 to 127, all different within a row; in each aligned block of 64 rows (0 to 63, 64 to 127, ..., all dimensions but the last counted through in order) at most 6 rows name the same one
- gate_proj: bfloat16 [128, 2048, 768], P(('seq', 'exp')), may hold values from -0.125 to 0.125
- up_proj: bfloat16 [128, 2048, 768], P(('seq', 'exp')), may hold values from -0.125 to 0.125
- down_proj: bfloat16 [128, 768, 2048], P(('seq', 'exp')), may hold values from -0.21875 to 0.21875
Outputs:
- layer_out: bfloat16 [16, 512, 2048], P('exp', 'seq')
The draws below stay inside these ranges and needn't reach their ends.
Inputs may be any that keep to these rules, and one draw needn't show every extreme that they name: `expert_ids`: among the rows of one device (aligned blocks of 64 tokens of one document) no expert is chosen more than 6 times; every token chooses 8 different experts. `cache_len`: some document fills its whole cache.
All inputs are finite; a program needn't handle non-finite values.
Results may differ from the reference program's by a relative error of at most 0.0042.
Values may be sent and summed in bfloat16 or wider, within the bound.
A program may use at most 128 MiB of HBM per device.

```python
import math
import jax
import jax.numpy as jnp
import numpy as np
from jax import lax

D = 2048
QH = 32
KVH = 4
HD = 128
F = 768
TOPK = 8
TOK_DEV = 64
EXPERTS = 128
DOCS = 16
QTOK = 512
CACHE = 4096
CAP = 6


def shared_draw(key):
    keys = jnp.clip(jax.random.normal(jax.random.fold_in(key, 11), (DOCS, CACHE, KVH * HD), jnp.float32), -6.0, 6.0)
    rows = jnp.clip(jax.random.normal(jax.random.fold_in(key, 12), (DOCS, QTOK, QH * HD), jnp.float32), -6.0, 6.0)
    return (keys, rows)


def draw_queries(key, part):
    return shared_draw(key)[1].astype(jnp.bfloat16)


def draw_cache_keys(key, part):
    return shared_draw(key)[0].astype(jnp.bfloat16)


def draw_cache_len(key, part):
    lengths = jax.random.randint(jax.random.fold_in(key, 3), (DOCS,), CACHE // 4, CACHE + 1)
    pick = jax.random.randint(jax.random.fold_in(key, 4), (), 0, DOCS)
    return lengths.at[pick].set(CACHE).astype(jnp.int32)


def shard_levels(rng, extent, split, smallest, top_value):
    factor_of, own = 1.0, jax.random.fold_in(rng, 6)
    for axis_at, blocks in split:
        steps = jnp.exp(jax.random.uniform(jax.random.fold_in(own, axis_at), (blocks,), jnp.float32, smallest / len(split), top_value / len(split)))
        factor_of = factor_of * jnp.repeat(steps, extent[axis_at] // blocks).reshape([-1 if axis == axis_at else 1 for axis in range(len(extent))])
    return factor_of


def shared_out(stream_key, own, number, rows, amount, top, bound, lean):
    order = jax.random.permutation(stream_key, amount)
    packed, common = shares(amount, rows * top, bound, lean, True), shares(amount, rows * top, bound, lean, False)
    places = jnp.arange(amount)

    def named(sizes, offset_by):
        used = int((sizes > 0).sum())
        fixed = max(1, used // 4)
        passed = fixed + (places - fixed + offset_by * (used - fixed)) % max(1, amount - fixed)
        return jnp.zeros((amount,), jnp.int32).at[order[jnp.where(places < fixed, places, passed)]].set(jnp.asarray(sizes, jnp.int32))

    sizes = jnp.where(number % 4 == 0, named(packed, number // 4), named(common, number - number // 4 - 1))
    mixed = jax.random.permutation(jax.random.fold_in(own, 3), amount)
    giver, taker = mixed[0:amount // 2 * 2:2], mixed[1:amount // 2 * 2:2]
    slack = jnp.minimum(sizes[giver] - 1, bound - sizes[taker]) // 2
    slack = jnp.where((giver == order[0]) | (taker == order[0]) | (sizes[taker] == 0), 0, jnp.maximum(slack, 0))
    passed = jax.random.randint(jax.random.fold_in(own, 4), (amount // 2,), 0, 1 << 20) % (slack + 1)
    sizes = sizes.at[giver].add(-passed).at[taker].add(passed)
    labels = jnp.searchsorted(jnp.cumsum(sizes), jnp.arange(rows * top), side="right").astype(jnp.int32)
    grid = labels.reshape(top, rows).T
    grid = grid[jax.random.permutation(jax.random.fold_in(own, 1), rows)]
    offset_by = jax.random.randint(jax.random.fold_in(own, 2), (rows, 1), 0, top)
    return jnp.take_along_axis(grid, (jnp.arange(top)[None, :] + offset_by) % top, axis=1)


def shares(number_of, total, bound, slope, full):
    loads = [(1 << 20) // math.isqrt(rank ** slope) + 1 for rank in range(1, number_of + 1)]
    largest = bound if full else min(bound, max(-(-total // number_of), total * loads[0] // sum(loads)))
    least = 1 if total - largest >= number_of - 1 else 0
    given, rest = [largest] + [least] * (number_of - 1), total - largest - least * (number_of - 1)
    while rest > 0:
        free = [i for i in range(1, number_of) if given[i] < largest] or [i for i in range(1, number_of) if given[i] < bound]
        pool, budget = sum([loads[i] for i in free]), rest
        for i in free:
            more = min(bound - given[i], max(1, budget * loads[i] // pool), rest)
            given[i] = given[i] + more
            rest = rest - more
    return np.array(given)


def scatter_about(stream_key, dims, scale, bound, shards=(), kind=jnp.bfloat16):
    array = jax.random.normal(stream_key, dims, jnp.float32) * scale
    if len(shards) > 0:
        array = shard_levels(stream_key, dims, shards, -0.22, 0.18) * array
    return jnp.clip(array, min=-bound, max=bound).astype(kind)


def setup_inputs(seed: int = 0) -> dict:
    key_list = jax.random.split(jax.random.key(seed), 15)
    queries = draw_queries(jax.random.fold_in(key_list[14], 71), 0)
    new_keys = scatter_about(key_list[1], (DOCS, QTOK, KVH * HD), 1.0, 6.0, ((0, 16), (1, 8)))
    new_values = scatter_about(key_list[2], (DOCS, QTOK, KVH * HD), 1.0, 6.0, ((0, 16), (1, 8)))
    cache_keys = draw_cache_keys(jax.random.fold_in(key_list[14], 71), 0)
    cache_values = scatter_about(key_list[4], (DOCS, CACHE, KVH * HD), 1.0, 6.0, ((0, 16), (1, 8)))
    cache_len = draw_cache_len(jax.random.fold_in(key_list[14], 71), 0)
    residual_in = scatter_about(key_list[6], (DOCS, QTOK, D), 1.0, 6.0, ((0, 16), (1, 8)))
    out_weight = scatter_about(key_list[7], (QH * HD, D), (QH * HD) ** -0.5, 0.09375, ((0, 8),))
    norm_gain = jnp.clip(1.0 + 0.15 * jax.random.normal(key_list[8], (D,), jnp.float32), 0.25, 1.75)
    router_weight = scatter_about(key_list[9], (D, EXPERTS), D ** -0.5, 0.125)
    expert_ids_keys = jax.random.split(jax.random.fold_in(key_list[10], 1), DOCS * QTOK // TOK_DEV)
    expert_ids_turns = jax.random.permutation(jax.random.fold_in(key_list[10], 3), DOCS * QTOK // TOK_DEV)
    expert_ids = jax.vmap(lambda own, number: shared_out(jax.random.fold_in(key_list[10], 2), own, number, TOK_DEV, EXPERTS, TOPK, CAP, 2))(expert_ids_keys, expert_ids_turns).reshape((DOCS, QTOK, TOPK))
    gate_proj = scatter_about(key_list[11], (EXPERTS, D, F), D ** -0.5, 0.125, ((0, 128),))
    up_proj = scatter_about(key_list[12], (EXPERTS, D, F), D ** -0.5, 0.125, ((0, 128),))
    down_proj = scatter_about(key_list[13], (EXPERTS, F, D), F ** -0.5, 0.21875, ((0, 128),))
    return {"queries": queries, "new_keys": new_keys, "new_values": new_values, "cache_keys": cache_keys, "cache_values": cache_values, "cache_len": cache_len, "residual_in": residual_in, "out_weight": out_weight, "norm_gain": norm_gain, "router_weight": router_weight, "expert_ids": expert_ids, "gate_proj": gate_proj, "up_proj": up_proj, "down_proj": down_proj}


def attend_doc(args):
    qrow, ckey, cval, nkey, nval, length = args
    group = QH // KVH
    total = CACHE + QTOK
    keys = jnp.concatenate([ckey, nkey], 0).reshape(total, KVH, HD).astype(jnp.float32)
    value_entries = jnp.concatenate([cval, nval], 0).reshape(total, KVH, HD).astype(jnp.float32)
    qheads = qrow.reshape(QTOK, KVH, group, HD).astype(jnp.float32)
    kpos = jnp.arange(total, dtype=jnp.int32)[None, :]
    qpos = jnp.arange(QTOK, dtype=jnp.int32)[:, None]
    visible = jnp.where(kpos < CACHE, kpos < length, kpos - CACHE <= qpos)

    def one_head(index_lookup):
        qsel = lax.dynamic_index_in_dim(qheads, index_lookup, 1, keepdims=False)
        ksel = lax.dynamic_index_in_dim(keys, index_lookup, 1, keepdims=False)
        selected_values = lax.dynamic_index_in_dim(value_entries, index_lookup, 1, keepdims=False)
        scores = jnp.einsum('qgd,kd->gqk', qsel, ksel) / jnp.sqrt(jnp.float32(HD))
        scores = jnp.where(visible[None], scores, jnp.float32(-1e+30))
        peak = lax.optimization_barrier(jnp.max(scores, axis=-1, keepdims=True))
        expo = jnp.exp(scores - peak)
        weight_matrices = (expo / lax.optimization_barrier(jnp.sum(expo, axis=-1, keepdims=True))).astype(jnp.bfloat16)
        return jnp.einsum('rxl,lc->xrc', weight_matrices.astype(jnp.float32), selected_values).astype(jnp.bfloat16)
    outs = lax.map(one_head, jnp.arange(KVH, dtype=jnp.int32))
    return jnp.transpose(outs, (1, 0, 2, 3)).reshape(QTOK, QH * HD)

def reference(queries, new_keys, new_values, cache_keys, cache_values, cache_len, residual_in, out_weight, norm_gain, router_weight, expert_ids, gate_proj, up_proj, down_proj):
    attn = lax.map(attend_doc, (queries, cache_keys, cache_values, new_keys, new_values, cache_len))
    count = DOCS * QTOK
    attn = attn.reshape(count, QH * HD)
    mixed = residual_in.reshape(count, D).astype(jnp.float32) + jnp.dot(attn, out_weight, preferred_element_type=jnp.float32)
    meansq = lax.optimization_barrier(jnp.mean(mixed * mixed, axis=-1, keepdims=True))
    normed = (mixed / jnp.sqrt(meansq + 1e-06) * norm_gain).astype(jnp.bfloat16)
    logits = jnp.dot(normed, router_weight, preferred_element_type=jnp.float32)
    chosen = expert_ids.reshape(count, TOPK)
    picked = jnp.take_along_axis(logits, chosen, axis=1)
    expo = jnp.exp(picked)
    gates = expo / lax.optimization_barrier(jnp.sum(expo, axis=1, keepdims=True))
    padded = jnp.concatenate([normed, jnp.zeros((1, D), jnp.bfloat16)], 0)
    slots = count // TOK_DEV * CAP

    def expert_step(acc, xs):
        wgate, wup, wdown, index_lookup = xs
        hit = chosen == index_lookup
        weight = lax.optimization_barrier(jnp.sum(jnp.where(hit, gates, jnp.float32(0.0)), axis=1))
        weight = jnp.concatenate([weight, jnp.zeros((1,), jnp.float32)], 0)
        rows = jnp.nonzero(jnp.any(hit, axis=1), size=slots, fill_value=count)[0].astype(jnp.int32)
        taken = padded[rows]
        gate = jnp.dot(taken, wgate, preferred_element_type=jnp.float32)
        upv = jnp.dot(taken, wup, preferred_element_type=jnp.float32)
        act = (jax.nn.silu(gate) * upv).astype(jnp.bfloat16)
        result = jnp.dot(act, wdown, preferred_element_type=jnp.float32).astype(jnp.bfloat16)
        acc = acc.at[rows].add(weight[rows][:, None] * result.astype(jnp.float32))
        return (acc, None)
    start = jnp.zeros((count + 1, D), jnp.float32)
    total, _ = lax.scan(expert_step, start, (gate_proj, up_proj, down_proj, jnp.arange(EXPERTS, dtype=jnp.int32)))
    out = mixed + total[:count]
    return out.astype(jnp.bfloat16).reshape(DOCS, QTOK, D)
```

```python
import jax
import jax.numpy as jnp
from jax import lax
from jax.experimental import pallas as pl
from jax.experimental.pallas import tpu as pltpu
from jax.sharding import PartitionSpec as P

QH = 32
KVH = 4
HD = 128
TOPK = 8
NSEQ = 8
TOK = 64
DOCTOK = 512
CDEV = 512
WIDTH = 2048
LOG2E = 1.4426950408889634
MESH = pl.DeviceIdType.MESH


def attention_kernel(
    len_ref, q_hbm, kn_hbm, vn_hbm, kc_hbm, vc_hbm, w_hbm, res_hbm, mixed_ref,
    qbuf, qext, kbuf, vbuf, acc, mbuf, wbuf, resbuf, part, sib_out, sib_in, x_out, x_in,
    loc_sem, kv_send, kv_recv, fw_send, fw_recv, q_send, q_recv, s_send, s_recv, x_send, x_recv,
):
    me = lax.axis_index("seq")
    ex = lax.axis_index("exp")
    x, c = me // 2, lax.rem(me, 2)
    other = 1 - c
    sibling = (2 * x + other, ex)

    def chip(d):
        return lax.rem(x + d, 4)

    barrier = pltpu.get_barrier_semaphore()
    for d in range(1, NSEQ):
        pl.semaphore_signal(
            barrier, inc=1, device_id=(lax.rem(me + d, NSEQ), ex), device_id_type=MESH
        )
    pl.semaphore_wait(barrier, NSEQ - 1)

    def rows_of(src):
        cached = pl.ds(pl.multiple_of(src * CDEV, CDEV), CDEV)
        fresh = pl.ds(pl.multiple_of(NSEQ * CDEV + src * TOK, TOK), TOK)
        return cached, fresh

    lanes = pl.ds(0, HD)

    def pieces(head, src):
        cols = pl.ds(pl.multiple_of(head * HD, HD), HD)
        cached, fresh = rows_of(src)
        return (
            (kc_hbm.at[:, cols], kbuf.at[cached, lanes]),
            (vc_hbm.at[:, cols], vbuf.at[cached, lanes]),
            (kn_hbm.at[:, cols], kbuf.at[fresh, lanes]),
            (vn_hbm.at[:, cols], vbuf.at[fresh, lanes]),
        )

    q_copies = []
    for d in (1, 2, 3, 5, 6, 7, 4):
        to = lax.rem(me + d, NSEQ)
        q_copies.append(pltpu.make_async_remote_copy(
            src_ref=q_hbm.at[:, pl.ds(pl.multiple_of(to * 512, 512), 512)],
            dst_ref=qbuf.at[pl.ds(pl.multiple_of(me * TOK, TOK), TOK), :],
            send_sem=q_send.at[d], recv_sem=q_recv.at[d],
            device_id=(to, ex), device_id_type=MESH,
        ))
    kv_copies = {}
    for d in (1, 3, 2):
        kv_copies[d] = [
            pltpu.make_async_remote_copy(
                src_ref=src, dst_ref=dst, send_sem=kv_send.at[d, i], recv_sem=kv_recv.at[d, i],
                device_id=(2 * chip(d) + c, ex), device_id_type=MESH,
            )
            for i, (src, dst) in enumerate(pieces(chip(d), me))
        ]
    fw_copies = {0: [
        pltpu.make_async_remote_copy(
            src_ref=src, dst_ref=dst, send_sem=fw_send.at[0, i], recv_sem=fw_recv.at[0, i],
            device_id=sibling, device_id_type=MESH,
        )
        for i, (src, dst) in enumerate(pieces(x, me))
    ]}
    local = [
        pltpu.make_async_copy(src, dst, loc_sem.at[i])
        for i, (src, dst) in enumerate(pieces(x, me))
    ]
    local.append(pltpu.make_async_copy(
        q_hbm.at[:, pl.ds(pl.multiple_of(me * 512, 512), 512)],
        qbuf.at[pl.ds(pl.multiple_of(me * TOK, TOK), TOK), :], loc_sem.at[4]))
    local.append(pltpu.make_async_copy(w_hbm, wbuf, loc_sem.at[5]))
    local.append(pltpu.make_async_copy(res_hbm, resbuf, loc_sem.at[6]))

    for cp in q_copies:
        cp.start()
    for cp in fw_copies[0]:
        cp.start()
    for cp in kv_copies[1] + kv_copies[3] + kv_copies[2]:
        cp.start()
    for cp in local:
        cp.start()

    total = NSEQ * (CDEV + TOK)
    upper = pl.ds(HD, HD)
    lane = lax.broadcasted_iota(jnp.int32, (total, HD), 1)
    pos = lax.broadcasted_iota(jnp.int32, (total, HD), 0)
    hidden = (pos >= len_ref[0]) & (pos < NSEQ * CDEV) & (lane == 0)
    kbuf[:, HD:] = jnp.where(hidden, jnp.float32(-1e30), jnp.float32(0.0)).astype(jnp.bfloat16)
    vbuf[:, HD:] = jnp.ones((total, HD), jnp.bfloat16)
    acc[...] = jnp.zeros_like(acc)
    mbuf[...] = jnp.full(mbuf.shape, -3e38, jnp.float32)

    for cp in q_copies:
        cp.wait_recv()
    local[4].wait()
    unit = (lax.broadcasted_iota(jnp.int32, (DOCTOK, HD), 1) == 0).astype(jnp.float32)
    for h in range(4):
        qext[h, :, :HD] = qbuf[:, h * HD:(h + 1) * HD]
        qext[h, :, HD:] = unit.astype(jnp.bfloat16)

    factor = jnp.float32(LOG2E / (HD ** 0.5))

    def attend(first, count, causal):
        keys_at = pl.ds(first, count)

        def one_head(h, carry):
            for half in range(2):
                rows = pl.ds(half * 256, 256)
                s = lax.dot_general(
                    qext[h, rows, :], kbuf[keys_at, :], (((1,), (1,)), ((), ())),
                    preferred_element_type=jnp.float32,
                )
                if causal:
                    t = lax.broadcasted_iota(jnp.int32, s.shape, 0) + half * 256
                    u = lax.broadcasted_iota(jnp.int32, s.shape, 1)
                    s = jnp.where(u <= t, s, jnp.float32(-1e30))
                m_old = mbuf[h, rows, :]
                m_new = jnp.maximum(m_old, jnp.max(s, axis=1, keepdims=True))
                mbuf[h, rows, :] = m_new
                alpha = jnp.exp2((m_old - m_new) * factor)
                p = jnp.exp2((s - m_new[:, :1]) * factor).astype(jnp.bfloat16)
                pv = jnp.dot(p, vbuf[keys_at, :], preferred_element_type=jnp.float32)
                acc[h, rows, :HD] = acc[h, rows, :HD] * alpha + pv[:, :HD]
                acc[h, rows, HD:] = acc[h, rows, HD:] * alpha + pv[:, HD:]
            return carry

        lax.fori_loop(0, 4, one_head, 0)

    for i in range(4):
        local[i].wait()
    for cp in fw_copies[0]:
        cp.wait_recv()
    attend(pl.multiple_of(x * 1024, 1024), 1024, False)
    for d in (1, 3, 2):
        for cp in kv_copies[d]:
            cp.wait_recv()
        src = 2 * lax.rem(x + 4 - d, 4) + c
        cached, fresh = rows_of(src)
        views = (kbuf.at[cached, lanes], vbuf.at[cached, lanes],
                 kbuf.at[fresh, lanes], vbuf.at[fresh, lanes])
        fw_copies[d] = [
            pltpu.make_async_remote_copy(
                src_ref=view, dst_ref=view, send_sem=fw_send.at[d, i], recv_sem=fw_recv.at[d, i],
                device_id=sibling, device_id_type=MESH,
            )
            for i, view in enumerate(views)
        ]
        for cp in fw_copies[d]:
            cp.start()
        for cp in fw_copies[d]:
            cp.wait_recv()
        attend(pl.multiple_of(lax.rem(x + 4 - d, 4) * 1024, 1024), 1024, False)
    attend(NSEQ * CDEV, DOCTOK, True)

    for h in range(4):
        qbuf[:, h * HD:(h + 1) * HD] = (acc[h, :, :HD] / acc[h, :, HD:]).astype(jnp.bfloat16)
    local[5].wait()

    sib_copies, x_copies = [], []
    for d in (2, 1, 3, 0):
        to = chip(d)
        theirs = pl.ds(pl.multiple_of((2 * to + other) * TOK, TOK), TOK)
        mine = pl.ds(pl.multiple_of((2 * to + c) * TOK, TOK), TOK)
        sib_out[d] = jnp.dot(
            qbuf[theirs, :], wbuf[...], preferred_element_type=jnp.float32
        ).astype(jnp.bfloat16)
        cp = pltpu.make_async_remote_copy(
            src_ref=sib_out.at[d], dst_ref=sib_in.at[d], send_sem=s_send.at[d],
            recv_sem=s_recv.at[d], device_id=sibling, device_id_type=MESH,
        )
        cp.start()
        sib_copies.append((d, cp))
        part[d] = jnp.dot(qbuf[mine, :], wbuf[...], preferred_element_type=jnp.float32)
    for d, cp in sib_copies:
        cp.wait_recv()
        if d:
            x_out[d] = (part[d] + sib_in[d].astype(jnp.float32)).astype(jnp.bfloat16)
            xcp = pltpu.make_async_remote_copy(
                src_ref=x_out.at[d], dst_ref=x_in.at[d], send_sem=x_send.at[d],
                recv_sem=x_recv.at[d], device_id=(2 * chip(d) + c, ex), device_id_type=MESH,
            )
            xcp.start()
            x_copies.append(xcp)
    local[6].wait()
    total_sum = resbuf[...].astype(jnp.float32) + part[0] + sib_in[0].astype(jnp.float32)
    for xcp in x_copies:
        xcp.wait_recv()
    for d in (1, 2, 3):
        total_sum = total_sum + x_in[d].astype(jnp.float32)
    mixed_ref[...] = total_sum

    for cp in q_copies + x_copies + [cp for _, cp in sib_copies]:
        cp.wait_send()
    for d in (0, 1, 2, 3):
        for cp in fw_copies[d]:
            cp.wait_send()
        if d:
            for cp in kv_copies[d]:
                cp.wait_send()


def attention_mixed(queries, new_keys, new_values, cache_keys, cache_values, cache_len, residual, out_weight):
    anyspec = pl.BlockSpec(memory_space=pl.ANY)
    total = NSEQ * (CDEV + TOK)
    bf, f32 = jnp.bfloat16, jnp.float32
    dma = pltpu.SemaphoreType.DMA
    return pl.pallas_call(
        attention_kernel,
        out_shape=jax.ShapeDtypeStruct((TOK, WIDTH), f32),
        in_specs=[pl.BlockSpec(memory_space=pltpu.SMEM)] + [anyspec] * 7,
        out_specs=pl.BlockSpec(memory_space=pltpu.VMEM),
        scratch_shapes=[
            pltpu.VMEM((DOCTOK, 512), bf),
            pltpu.VMEM((4, DOCTOK, 256), bf),
            pltpu.VMEM((total, 256), bf),
            pltpu.VMEM((total, 256), bf),
            pltpu.VMEM((4, DOCTOK, 256), f32),
            pltpu.VMEM((4, DOCTOK, HD), f32),
            pltpu.VMEM((512, WIDTH), bf),
            pltpu.VMEM((TOK, WIDTH), bf),
            pltpu.VMEM((4, TOK, WIDTH), f32),
            pltpu.VMEM((4, TOK, WIDTH), bf),
            pltpu.VMEM((4, TOK, WIDTH), bf),
            pltpu.VMEM((4, TOK, WIDTH), bf),
            pltpu.VMEM((4, TOK, WIDTH), bf),
            dma((7,)), dma((4, 4)), dma((4, 4)), dma((4, 4)), dma((4, 4)),
            dma((8,)), dma((8,)), dma((4,)), dma((4,)), dma((4,)), dma((4,)),
        ],
        compiler_params=pltpu.CompilerParams(
            collective_id=0, has_side_effects=True, vmem_limit_bytes=56 * 2**20
        ),
        name="attention_exchange",
    )(cache_len, queries[0], new_keys[0], new_values[0], cache_keys[0], cache_values[0],
      out_weight, residual[0])


def expert_token_rows(piece, gate_proj, up_proj, down_proj):
    width = piece.shape[-1]
    rows = piece.reshape(-1, width)
    gate = jnp.dot(rows, gate_proj[0], preferred_element_type=jnp.float32)
    upv = jnp.dot(rows, up_proj[0], preferred_element_type=jnp.float32)
    act = (jax.nn.silu(gate) * upv).astype(jnp.bfloat16)
    result = jnp.dot(act, down_proj[0], preferred_element_type=jnp.float32).astype(jnp.bfloat16)
    return result.reshape(piece.shape)


def body(
    queries,
    new_keys,
    new_values,
    cache_keys,
    cache_values,
    cache_len,
    residual_in,
    out_weight,
    norm_gain,
    router_weight,
    expert_ids,
    gate_proj,
    up_proj,
    down_proj,
):
    tokens = queries.shape[1]
    width = residual_in.shape[2]
    mixed = attention_mixed(
        queries, new_keys, new_values, cache_keys, cache_values, cache_len, residual_in, out_weight
    )
    meansq = jnp.mean(mixed * mixed, axis=-1, keepdims=True)
    normed = (mixed / jnp.sqrt(meansq + 1e-06) * norm_gain).astype(jnp.bfloat16)
    logits = jnp.dot(normed, router_weight, preferred_element_type=jnp.float32)
    nexp = router_weight.shape[1]
    chosen = expert_ids[0]
    onehot = chosen[:, :, None] == jnp.arange(nexp, dtype=jnp.int32)[None, None, :]
    picked = jnp.sum(jnp.where(onehot, logits[:, None, :], jnp.float32(0.0)), axis=2)
    expo = jnp.exp(picked)
    gates = expo / jnp.sum(expo, axis=1, keepdims=True)
    capacity = 3 * tokens * TOPK // (2 * nexp)
    flat = chosen.reshape(-1)
    member = (flat[:, None] == jnp.arange(nexp, dtype=jnp.int32)[None, :]).astype(jnp.int32)
    rank = jnp.sum((jnp.cumsum(member, axis=0) - 1) * member, axis=1)
    slot = flat * capacity + rank
    place = slot[:, None] == jnp.arange(nexp * capacity, dtype=jnp.int32)[None, :]
    route = jnp.any(place.reshape(tokens, TOPK, nexp * capacity), axis=1).astype(jnp.bfloat16)
    packed = jnp.einsum("ts,td->sd", route, normed, preferred_element_type=jnp.float32).astype(
        jnp.bfloat16
    )
    outgoing = packed.reshape(nexp, capacity, width)
    result = expert_token_rows(
        lax.all_to_all(outgoing, ("seq", "exp"), split_axis=0, concat_axis=0, tiled=True),
        gate_proj,
        up_proj,
        down_proj,
    )
    back = lax.all_to_all(result, ("seq", "exp"), split_axis=0, concat_axis=0, tiled=True)
    back = back.reshape(nexp * capacity, width)
    gathered = back[slot].reshape(tokens, TOPK, width)
    moe = jnp.sum(gates[:, :, None] * gathered.astype(jnp.float32), axis=1)
    return (mixed + moe).astype(jnp.bfloat16).reshape(1, tokens, width)


def solution(mesh):
    in_specs = (
        P("exp", "seq", None),
        P("exp", "seq", None),
        P("exp", "seq", None),
        P("exp", "seq", None),
        P("exp", "seq", None),
        P("exp"),
        P("exp", "seq", None),
        P("seq", None),
        P(),
        P(),
        P("exp", "seq", None),
        P(("seq", "exp"), None, None),
        P(("seq", "exp"), None, None),
        P(("seq", "exp"), None, None),
    )
    out_specs = P("exp", "seq", None)
    return jax.shard_map(body, mesh=mesh, in_specs=in_specs, out_specs=out_specs, check_vma=False)
```

```python
import jax
import jax.numpy as jnp
from jax import lax
from jax.experimental import pallas as pl
from jax.experimental.pallas import tpu as pltpu
from jax.sharding import PartitionSpec as P

QH = 32
KVH = 4
HD = 128
TOPK = 8
NSEQ = 8
TOK = 64
DOCTOK = 512
CDEV = 512
WIDTH = 2048
LOG2E = 1.4426950408889634
MESH = pl.DeviceIdType.MESH


def attention_kernel(
    len_ref, q_hbm, kn_hbm, vn_hbm, kc_hbm, vc_hbm, w_hbm, res_hbm, mixed_ref,
    qbuf, qext, kbuf, vbuf, acc, mbuf, wbuf, resbuf, part, sib_out, sib_in, x_out, x_in,
    loc_sem, kv_send, kv_recv, fw_send, fw_recv, q_send, q_recv, s_send, s_recv, x_send, x_recv,
):
    me = lax.axis_index("seq")
    ex = lax.axis_index("exp")
    x, c = me // 2, lax.rem(me, 2)
    other = 1 - c
    sibling = (2 * x + other, ex)

    def chip(d):
        return lax.rem(x + d, 4)

    barrier = pltpu.get_barrier_semaphore()
    for d in range(1, NSEQ):
        pl.semaphore_signal(
            barrier, inc=1, device_id=(lax.rem(me + d, NSEQ), ex), device_id_type=MESH
        )
    pl.semaphore_wait(barrier, NSEQ - 1)

    def rows_of(src):
        cached = pl.ds(pl.multiple_of(src * CDEV, CDEV), CDEV)
        fresh = pl.ds(pl.multiple_of(NSEQ * CDEV + src * TOK, TOK), TOK)
        return cached, fresh

    lanes = pl.ds(0, HD)

    def pieces(head, src):
        cols = pl.ds(pl.multiple_of(head * HD, HD), HD)
        cached, fresh = rows_of(src)
        return (
            (kc_hbm.at[:, cols], kbuf.at[cached, lanes]),
            (vc_hbm.at[:, cols], vbuf.at[cached, lanes]),
            (kn_hbm.at[:, cols], kbuf.at[fresh, lanes]),
            (vn_hbm.at[:, cols], vbuf.at[fresh, lanes]),
        )

    q_copies = []
    for d in (1, 2, 3, 5, 6, 7, 4):
        to = lax.rem(me + d, NSEQ)
        q_copies.append(pltpu.make_async_remote_copy(
            src_ref=q_hbm.at[:, pl.ds(pl.multiple_of(to * 512, 512), 512)],
            dst_ref=qbuf.at[pl.ds(pl.multiple_of(me * TOK, TOK), TOK), :],
            send_sem=q_send.at[d], recv_sem=q_recv.at[d],
            device_id=(to, ex), device_id_type=MESH,
        ))
    kv_copies = {}
    for d in (1, 3, 2):
        kv_copies[d] = [
            pltpu.make_async_remote_copy(
                src_ref=src, dst_ref=dst, send_sem=kv_send.at[d, i], recv_sem=kv_recv.at[d, i],
                device_id=(2 * chip(d) + c, ex), device_id_type=MESH,
            )
            for i, (src, dst) in enumerate(pieces(chip(d), me))
        ]
    fw_copies = {0: [
        pltpu.make_async_remote_copy(
            src_ref=src, dst_ref=dst, send_sem=fw_send.at[0, i], recv_sem=fw_recv.at[0, i],
            device_id=sibling, device_id_type=MESH,
        )
        for i, (src, dst) in enumerate(pieces(x, me))
    ]}
    local = [
        pltpu.make_async_copy(src, dst, loc_sem.at[i])
        for i, (src, dst) in enumerate(pieces(x, me))
    ]
    local.append(pltpu.make_async_copy(
        q_hbm.at[:, pl.ds(pl.multiple_of(me * 512, 512), 512)],
        qbuf.at[pl.ds(pl.multiple_of(me * TOK, TOK), TOK), :], loc_sem.at[4]))
    local.append(pltpu.make_async_copy(w_hbm, wbuf, loc_sem.at[5]))
    local.append(pltpu.make_async_copy(res_hbm, resbuf, loc_sem.at[6]))

    for cp in q_copies:
        cp.start()
    for cp in fw_copies[0]:
        cp.start()
    for cp in kv_copies[1] + kv_copies[3] + kv_copies[2]:
        cp.start()
    for cp in local:
        cp.start()

    total = NSEQ * (CDEV + TOK)
    upper = pl.ds(HD, HD)
    lane = lax.broadcasted_iota(jnp.int32, (total, HD), 1)
    pos = lax.broadcasted_iota(jnp.int32, (total, HD), 0)
    hidden = (pos >= len_ref[0]) & (pos < NSEQ * CDEV) & (lane == 0)
    kbuf[:, HD:] = jnp.where(hidden, jnp.float32(-1e30), jnp.float32(0.0)).astype(jnp.bfloat16)
    vbuf[:, HD:] = jnp.ones((total, HD), jnp.bfloat16)
    acc[...] = jnp.zeros_like(acc)
    mbuf[...] = jnp.full(mbuf.shape, -3e38, jnp.float32)

    for cp in q_copies:
        cp.wait_recv()
    local[4].wait()
    unit = (lax.broadcasted_iota(jnp.int32, (DOCTOK, HD), 1) == 0).astype(jnp.float32)
    for h in range(4):
        qext[h, :, :HD] = qbuf[:, h * HD:(h + 1) * HD]
        qext[h, :, HD:] = unit.astype(jnp.bfloat16)

    factor = jnp.float32(LOG2E / (HD ** 0.5))

    def attend(first, count, causal):
        keys_at = pl.ds(first, count)

        def one_head(h, carry):
            for half in range(2):
                rows = pl.ds(half * 256, 256)
                s = lax.dot_general(
                    qext[h, rows, :], kbuf[keys_at, :], (((1,), (1,)), ((), ())),
                    preferred_element_type=jnp.float32,
                )
                if causal:
                    t = lax.broadcasted_iota(jnp.int32, s.shape, 0) + half * 256
                    u = lax.broadcasted_iota(jnp.int32, s.shape, 1)
                    s = jnp.where(u <= t, s, jnp.float32(-1e30))
                m_old = mbuf[h, rows, :]
                m_new = jnp.maximum(m_old, jnp.max(s, axis=1, keepdims=True))
                mbuf[h, rows, :] = m_new
                alpha = jnp.exp2((m_old - m_new) * factor)
                p = jnp.exp2((s - m_new[:, :1]) * factor).astype(jnp.bfloat16)
                pv = jnp.dot(p, vbuf[keys_at, :], preferred_element_type=jnp.float32)
                acc[h, rows, :HD] = acc[h, rows, :HD] * alpha + pv[:, :HD]
                acc[h, rows, HD:] = acc[h, rows, HD:] * alpha + pv[:, HD:]
            return carry

        lax.fori_loop(0, 4, one_head, 0)

    for i in range(4):
        local[i].wait()
    for cp in fw_copies[0]:
        cp.wait_recv()
    attend(pl.multiple_of(x * 1024, 1024), 1024, False)
    for d in (1, 3, 2):
        for cp in kv_copies[d]:
            cp.wait_recv()
        src = 2 * lax.rem(x + 4 - d, 4) + c
        cached, fresh = rows_of(src)
        views = (kbuf.at[cached, lanes], vbuf.at[cached, lanes],
                 kbuf.at[fresh, lanes], vbuf.at[fresh, lanes])
        fw_copies[d] = [
            pltpu.make_async_remote_copy(
                src_ref=view, dst_ref=view, send_sem=fw_send.at[d, i], recv_sem=fw_recv.at[d, i],
                device_id=sibling, device_id_type=MESH,
            )
            for i, view in enumerate(views)
        ]
        for cp in fw_copies[d]:
            cp.start()
        for cp in fw_copies[d]:
            cp.wait_recv()
        attend(pl.multiple_of(lax.rem(x + 4 - d, 4) * 1024, 1024), 1024, False)
    attend(NSEQ * CDEV, DOCTOK, True)

    for h in range(4):
        qbuf[:, h * HD:(h + 1) * HD] = (acc[h, :, :HD] / acc[h, :, HD:]).astype(jnp.bfloat16)
    local[5].wait()

    sib_copies, x_copies = [], []
    for d in (2, 1, 3, 0):
        to = chip(d)
        theirs = pl.ds(pl.multiple_of((2 * to + other) * TOK, TOK), TOK)
        mine = pl.ds(pl.multiple_of((2 * to + c) * TOK, TOK), TOK)
        sib_out[d] = jnp.dot(
            qbuf[theirs, :], wbuf[...], preferred_element_type=jnp.float32
        ).astype(jnp.bfloat16)
        cp = pltpu.make_async_remote_copy(
            src_ref=sib_out.at[d], dst_ref=sib_in.at[d], send_sem=s_send.at[d],
            recv_sem=s_recv.at[d], device_id=sibling, device_id_type=MESH,
        )
        cp.start()
        sib_copies.append((d, cp))
        part[d] = jnp.dot(qbuf[mine, :], wbuf[...], preferred_element_type=jnp.float32)
    for d, cp in sib_copies:
        cp.wait_recv()
        if d:
            x_out[d] = (part[d] + sib_in[d].astype(jnp.float32)).astype(jnp.bfloat16)
            xcp = pltpu.make_async_remote_copy(
                src_ref=x_out.at[d], dst_ref=x_in.at[d], send_sem=x_send.at[d],
                recv_sem=x_recv.at[d], device_id=(2 * chip(d) + c, ex), device_id_type=MESH,
            )
            xcp.start()
            x_copies.append(xcp)
    local[6].wait()
    total_sum = resbuf[...].astype(jnp.float32) + part[0] + sib_in[0].astype(jnp.float32)
    for xcp in x_copies:
        xcp.wait_recv()
    for d in (1, 2, 3):
        total_sum = total_sum + x_in[d].astype(jnp.float32)
    mixed_ref[...] = total_sum

    for cp in q_copies + x_copies + [cp for _, cp in sib_copies]:
        cp.wait_send()
    for d in (0, 1, 2, 3):
        for cp in fw_copies[d]:
            cp.wait_send()
        if d:
            for cp in kv_copies[d]:
                cp.wait_send()


def attention_mixed(queries, new_keys, new_values, cache_keys, cache_values, cache_len, residual, out_weight):
    anyspec = pl.BlockSpec(memory_space=pl.ANY)
    total = NSEQ * (CDEV + TOK)
    bf, f32 = jnp.bfloat16, jnp.float32
    dma = pltpu.SemaphoreType.DMA
    return pl.pallas_call(
        attention_kernel,
        out_shape=jax.ShapeDtypeStruct((TOK, WIDTH), f32),
        in_specs=[pl.BlockSpec(memory_space=pltpu.SMEM)] + [anyspec] * 7,
        out_specs=pl.BlockSpec(memory_space=pltpu.VMEM),
        scratch_shapes=[
            pltpu.VMEM((DOCTOK, 512), bf),
            pltpu.VMEM((4, DOCTOK, 256), bf),
            pltpu.VMEM((total, 256), bf),
            pltpu.VMEM((total, 256), bf),
            pltpu.VMEM((4, DOCTOK, 256), f32),
            pltpu.VMEM((4, DOCTOK, HD), f32),
            pltpu.VMEM((512, WIDTH), bf),
            pltpu.VMEM((TOK, WIDTH), bf),
            pltpu.VMEM((4, TOK, WIDTH), f32),
            pltpu.VMEM((4, TOK, WIDTH), bf),
            pltpu.VMEM((4, TOK, WIDTH), bf),
            pltpu.VMEM((4, TOK, WIDTH), bf),
            pltpu.VMEM((4, TOK, WIDTH), bf),
            dma((7,)), dma((4, 4)), dma((4, 4)), dma((4, 4)), dma((4, 4)),
            dma((8,)), dma((8,)), dma((4,)), dma((4,)), dma((4,)), dma((4,)),
        ],
        compiler_params=pltpu.CompilerParams(
            collective_id=0, has_side_effects=True, vmem_limit_bytes=56 * 2**20
        ),
        name="attention_exchange",
    )(cache_len, queries[0], new_keys[0], new_values[0], cache_keys[0], cache_values[0],
      out_weight, residual[0])


EXPERTS = 128
FF = 768
PEERS = 16
SLOTS = 48
CAP = 6
ROWS = PEERS * SLOTS
NCHUNK = 4
CHUNK = WIDTH // NCHUNK


def experts_kernel(
    mixed_hbm, gain_ref, router_ref, ids_ref, wg_hbm, wu_hbm, wd_hbm, out_ref,
    mixed, tokens, table, pick, give, outbox, inbox, wg, wu, wd, hg, hu, act,
    results, back, part, sib_out, sib_in, x_out, x_in,
    loc_sem, t_send, t_recv, a_send, a_recv, f_send, f_recv, d_send, d_recv, r_send, r_recv,
    s_send, s_recv, x_send, x_recv,
):
    me = lax.axis_index("seq")
    ex = lax.axis_index("exp")
    x, c = me // 2, lax.rem(me, 2)
    other = 1 - c
    sibling = (2 * x + other, ex)
    f32, bf = jnp.float32, jnp.bfloat16

    def chip(d):
        return lax.rem(x + d, 4)

    def peer(d):
        return (me, plane_index(ex, d))

    loads = [
        pltpu.make_async_copy(mixed_hbm, mixed, loc_sem.at[0]),
        pltpu.make_async_copy(wg_hbm, wg, loc_sem.at[1]),
        pltpu.make_async_copy(wu_hbm, wu, loc_sem.at[2]),
        pltpu.make_async_copy(wd_hbm, wd, loc_sem.at[3]),
    ]
    for cp in loads:
        cp.start()
    barrier = pltpu.get_barrier_semaphore()
    for d in range(1, NSEQ):
        pl.semaphore_signal(
            barrier, inc=1, device_id=(lax.rem(me + d, NSEQ), ex), device_id_type=MESH
        )
    for d in range(1, PEERS):
        pl.semaphore_signal(barrier, inc=1, device_id=peer(d), device_id_type=MESH)
    loads[0].wait()

    def block(s):
        return pl.ds(pl.multiple_of(s * TOK, TOK), TOK)

    def group(e):
        return pl.ds(pl.multiple_of(e * SLOTS, 16), SLOTS)

    def span(k):
        return pl.ds(k * CHUNK, CHUNK)

    mx = mixed[...]
    meansq = jnp.mean(mx * mx, axis=1, keepdims=True)
    normed = (mx / jnp.sqrt(meansq + 1e-06) * gain_ref[...]).astype(bf)
    tokens[block(me), :] = normed
    pl.semaphore_wait(barrier, NSEQ - 1 + PEERS - 1)

    a_copies = {}
    for k in range(NCHUNK):
        for d in (0, 2, 1, 3):
            to = sibling if d == 0 else (2 * chip(d) + c, ex)
            view = tokens.at[block(me), span(k)]
            cp = pltpu.make_async_remote_copy(
                src_ref=view, dst_ref=view, send_sem=a_send.at[k, d], recv_sem=a_recv.at[k, d],
                device_id=to, device_id_type=MESH,
            )
            cp.start()
            a_copies[k, d] = cp

    logits = jnp.dot(normed, router_ref[...], preferred_element_type=f32)
    lane = lax.broadcasted_iota(jnp.int32, (TOK, EXPERTS), 1)
    chosen = jnp.zeros((TOK, EXPERTS), f32)
    for k in range(TOPK):
        chosen = chosen + jnp.where(ids_ref[:, k:k + 1] == lane, f32(1.0), f32(0.0))
    expo = jnp.where(chosen > 0, jnp.exp(logits), f32(0.0))
    gates = expo / jnp.sum(expo, axis=1, keepdims=True)
    before = (lax.broadcasted_iota(jnp.int32, (TOK, TOK), 1)
              < lax.broadcasted_iota(jnp.int32, (TOK, TOK), 0)).astype(f32)
    rank = jnp.dot(before.astype(bf), chosen.astype(bf), preferred_element_type=f32)
    first = (CAP * me + 1).astype(f32)
    place = jnp.where(chosen > 0, rank + first, f32(0.0))
    table[block(me), :EXPERTS] = place.astype(bf)
    table[block(me), EXPERTS:] = gates.astype(bf)
    t_copies = []
    for d in range(1, NSEQ):
        view = table.at[block(me), :]
        cp = pltpu.make_async_remote_copy(
            src_ref=view, dst_ref=view, send_sem=t_send.at[d], recv_sem=t_recv.at[d],
            device_id=(lax.rem(me + d, NSEQ), ex), device_id_type=MESH,
        )
        cp.start()
        t_copies.append(cp)

    f_copies = {}

    def forward(k):
        for d in (2, 1, 3):
            a_copies[k, d].wait_recv()
            view = tokens.at[block(2 * lax.rem(x + 4 - d, 4) + c), span(k)]
            cp = pltpu.make_async_remote_copy(
                src_ref=view, dst_ref=view, send_sem=f_send.at[k, d], recv_sem=f_recv.at[k, d],
                device_id=sibling, device_id_type=MESH,
            )
            cp.start()
            f_copies[k, d] = cp

    for cp in t_copies:
        cp.wait_recv()
    qi = lax.broadcasted_iota(jnp.int32, (ROWS, EXPERTS), 0)
    ei = (lax.broadcasted_iota(jnp.int32, (ROWS, EXPERTS), 1) - me * PEERS) * SLOTS
    owner = jnp.where((qi >= ei) & (qi < ei + SLOTS), f32(1.0), f32(0.0)).astype(bf)
    nt = (((1,), (1,)), ((), ()))

    def within(shape, axis):
        at = lax.broadcasted_iota(jnp.int32, shape, axis)
        low = at + 1
        for e in range(1, PEERS):
            low = jnp.where(at >= e * SLOTS, at + 1 - e * SLOTS, low)
        return low.astype(f32)

    codes, shares = table[:, :EXPERTS], table[:, EXPERTS:]
    by_row = lax.dot_general(owner, codes, nt, preferred_element_type=f32)
    pick[...] = jnp.where(by_row == within((ROWS, 128), 0)[:, :1], f32(1.0), f32(0.0)).astype(bf)
    by_token = lax.dot_general(codes, owner, nt, preferred_element_type=f32)
    spread = lax.dot_general(shares, owner, nt, preferred_element_type=f32)
    give[...] = jnp.where(by_token == within((8, ROWS), 1)[:1, :], spread, f32(0.0)).astype(bf)

    d_copies, r_copies = {}, {}
    for k in range(NCHUNK):
        forward(k)
        a_copies[k, 0].wait_recv()
        for d in (2, 1, 3):
            f_copies[k, d].wait_recv()
        outbox[:, span(k)] = jnp.dot(
            pick[...], tokens[:, span(k)], preferred_element_type=f32
        ).astype(bf)
        for d in PLANE_ORDER:
            to = plane_index(ex, d)
            cp = pltpu.make_async_remote_copy(
                src_ref=outbox.at[group(to), span(k)], dst_ref=inbox.at[group(ex), span(k)],
                send_sem=d_send.at[k, d], recv_sem=d_recv.at[k, d],
                device_id=(me, to), device_id_type=MESH,
            )
            cp.start()
            d_copies[k, d] = cp
        inbox[group(ex), span(k)] = outbox[group(ex), span(k)]

    loads[1].wait()
    loads[2].wait()
    for k in range(NCHUNK):
        for d in PLANE_ORDER:
            d_copies[k, d].wait_recv()
        rows = inbox[:, span(k)]
        g = jnp.dot(rows, wg[span(k), :], preferred_element_type=f32)
        u = jnp.dot(rows, wu[span(k), :], preferred_element_type=f32)
        if k == 0:
            hg[...] = g
            hu[...] = u
        elif k < NCHUNK - 1:
            hg[...] += g
            hu[...] += u
        else:
            g = hg[...] + g
            u = hu[...] + u
            act[...] = (g / (f32(1.0) + jnp.exp(-g)) * u).astype(bf)
    loads[3].wait()
    for k in range(NCHUNK):
        results[:, span(k)] = jnp.dot(
            act[...], wd[:, span(k)], preferred_element_type=f32
        ).astype(bf)
        for d in PLANE_ORDER:
            to = plane_index(ex, d)
            cp = pltpu.make_async_remote_copy(
                src_ref=results.at[group(to), span(k)], dst_ref=back.at[group(ex), span(k)],
                send_sem=r_send.at[k, d], recv_sem=r_recv.at[k, d],
                device_id=(me, to), device_id_type=MESH,
            )
            cp.start()
            r_copies[k, d] = cp
        back[group(ex), span(k)] = results[group(ex), span(k)]

    s_copies, x_copies = {}, {}

    def reduce_chips(k):
        for d in (2, 1, 3, 0):
            s_copies[k, d].wait_recv()
            if d:
                x_out[d, :, span(k)] = (
                    part[d, :, span(k)] + sib_in[d, :, span(k)].astype(f32)
                ).astype(bf)
                cp = pltpu.make_async_remote_copy(
                    src_ref=x_out.at[d, :, span(k)], dst_ref=x_in.at[d, :, span(k)],
                    send_sem=x_send.at[k, d], recv_sem=x_recv.at[k, d],
                    device_id=(2 * chip(d) + c, ex), device_id_type=MESH,
                )
                cp.start()
                x_copies[k, d] = cp

    for k in range(NCHUNK):
        for d in PLANE_ORDER:
            r_copies[k, d].wait_recv()
        for d in (2, 1, 3, 0):
            to = chip(d)
            sib_out[d, :, span(k)] = jnp.dot(
                give[block(2 * to + other), :], back[:, span(k)], preferred_element_type=f32
            ).astype(bf)
            cp = pltpu.make_async_remote_copy(
                src_ref=sib_out.at[d, :, span(k)], dst_ref=sib_in.at[d, :, span(k)],
                send_sem=s_send.at[k, d], recv_sem=s_recv.at[k, d],
                device_id=sibling, device_id_type=MESH,
            )
            cp.start()
            s_copies[k, d] = cp
            part[d, :, span(k)] = jnp.dot(
                give[block(2 * to + c), :], back[:, span(k)], preferred_element_type=f32
            )
        if k:
            reduce_chips(k - 1)
    reduce_chips(NCHUNK - 1)
    for k in range(NCHUNK):
        total = mixed[:, span(k)] + part[0, :, span(k)] + sib_in[0, :, span(k)].astype(f32)
        for d in (1, 2, 3):
            x_copies[k, d].wait_recv()
        for d in (1, 2, 3):
            total = total + x_in[d, :, span(k)].astype(f32)
        out_ref[:, span(k)] = total.astype(bf)

    for group_of in (a_copies, f_copies, d_copies, r_copies, s_copies, x_copies):
        for cp in group_of.values():
            cp.wait_send()
    for cp in t_copies:
        cp.wait_send()


PLANE_ORDER = tuple(range(1, PEERS))


def plane_index(ex, d):
    y, z = ex // 4, lax.rem(ex, 4)
    return lax.rem(y + d // 4, 4) * 4 + lax.rem(z + d % 4, 4)


def experts_layer(mixed, gain, router, ids, gate_proj, up_proj, down_proj):
    anyspec = pl.BlockSpec(memory_space=pl.ANY)
    vmem = pl.BlockSpec(memory_space=pltpu.VMEM)
    bf, f32 = jnp.bfloat16, jnp.float32
    dma = pltpu.SemaphoreType.DMA
    return pl.pallas_call(
        experts_kernel,
        out_shape=jax.ShapeDtypeStruct((TOK, WIDTH), bf),
        in_specs=[anyspec, vmem, vmem, vmem, anyspec, anyspec, anyspec],
        out_specs=vmem,
        scratch_shapes=[
            pltpu.VMEM((TOK, WIDTH), f32),
            pltpu.VMEM((DOCTOK, WIDTH), bf),
            pltpu.VMEM((DOCTOK, 2 * EXPERTS), bf),
            pltpu.VMEM((ROWS, DOCTOK), bf),
            pltpu.VMEM((DOCTOK, ROWS), bf),
            pltpu.VMEM((ROWS, WIDTH), bf),
            pltpu.VMEM((ROWS, WIDTH), bf),
            pltpu.VMEM((WIDTH, FF), bf),
            pltpu.VMEM((WIDTH, FF), bf),
            pltpu.VMEM((FF, WIDTH), bf),
            pltpu.VMEM((ROWS, FF), f32),
            pltpu.VMEM((ROWS, FF), f32),
            pltpu.VMEM((ROWS, FF), bf),
            pltpu.VMEM((ROWS, WIDTH), bf),
            pltpu.VMEM((ROWS, WIDTH), bf),
            pltpu.VMEM((4, TOK, WIDTH), f32),
            pltpu.VMEM((4, TOK, WIDTH), bf),
            pltpu.VMEM((4, TOK, WIDTH), bf),
            pltpu.VMEM((4, TOK, WIDTH), bf),
            pltpu.VMEM((4, TOK, WIDTH), bf),
            dma((4,)), dma((8,)), dma((8,)),
            dma((NCHUNK, 4)), dma((NCHUNK, 4)), dma((NCHUNK, 4)), dma((NCHUNK, 4)),
            dma((NCHUNK, 16)), dma((NCHUNK, 16)), dma((NCHUNK, 16)), dma((NCHUNK, 16)),
            dma((NCHUNK, 4)), dma((NCHUNK, 4)), dma((NCHUNK, 4)), dma((NCHUNK, 4)),
        ],
        compiler_params=pltpu.CompilerParams(
            collective_id=1, has_side_effects=True, vmem_limit_bytes=60 * 2**20
        ),
        name="experts_exchange",
    )(mixed, gain.reshape(1, WIDTH), router, ids, gate_proj[0], up_proj[0], down_proj[0])


def body(
    queries, new_keys, new_values, cache_keys, cache_values, cache_len, residual_in,
    out_weight, norm_gain, router_weight, expert_ids, gate_proj, up_proj, down_proj,
):
    mixed = attention_mixed(
        queries, new_keys, new_values, cache_keys, cache_values, cache_len, residual_in, out_weight
    )
    out = experts_layer(
        mixed, norm_gain, router_weight, expert_ids[0], gate_proj, up_proj, down_proj
    )
    return out.reshape(1, TOK, WIDTH)


def solution(mesh):
    in_specs = (
        P("exp", "seq", None),
        P("exp", "seq", None),
        P("exp", "seq", None),
        P("exp", "seq", None),
        P("exp", "seq", None),
        P("exp"),
        P("exp", "seq", None),
        P("seq", None),
        P(),
        P(),
        P("exp", "seq", None),
        P(("seq", "exp"), None, None),
        P(("seq", "exp"), None, None),
        P(("seq", "exp"), None, None),
    )
    out_specs = P("exp", "seq", None)
    return jax.shard_map(body, mesh=mesh, in_specs=in_specs, out_specs=out_specs, check_vma=False)
```

```python
import jax
import jax.numpy as jnp
from jax import lax
from jax.experimental import pallas as pl
from jax.experimental.pallas import tpu as pltpu
from jax.sharding import PartitionSpec as P

QH = 32
KVH = 4
HD = 128
TOPK = 8
NSEQ = 8
TOK = 64
DOCTOK = 512
CDEV = 512
WIDTH = 2048
LOG2E = 1.4426950408889634
MESH = pl.DeviceIdType.MESH


EXPERTS = 128
FF = 768
PEERS = 16
SLOTS = 48
CAP = 6
ROWS = PEERS * SLOTS
NCHUNK = 4
CHUNK = WIDTH // NCHUNK
NT = (((1,), (1,)), ((), ()))


def layer_kernel(
    len_ref, ids_ref, gain_ref, q_hbm, kn_hbm, vn_hbm, kc_hbm, vc_hbm, w_hbm, res_hbm,
    router_hbm, wg_hbm, wu_hbm, wd_hbm, out_ref,
    qbuf, qext, kbuf, vbuf, acc, mbuf, attn, wbuf, resbuf, router, part,
    sib_out, sib_in, x_out, x_in, sib_in2, x_in2,
    mixed, tokens, table, gtable, pick, give, outbox, relay_out, inbox, relay_back, back,
    rbox, rrelay, rin, wg, wu, wd, hg, hu, act,
    loc_sem, c_send, c_recv, q_send, q_recv, n_send, n_recv, kv_send, kv_recv, fw_send, fw_recv,
    s_send, s_recv, x_send, x_recv, a_send, a_recv, f_send, f_recv, g_send, g_recv,
    d_send, d_recv, r_send, r_recv, s2_send, s2_recv, x2_send, x2_recv,
):
    me = lax.axis_index("seq")
    ex = lax.axis_index("exp")
    x, c = me // 2, lax.rem(me, 2)
    y, z = ex // 4, lax.rem(ex, 4)
    other = 1 - c
    sibling = (2 * x + other, ex)
    f32, bf = jnp.float32, jnp.bfloat16
    everything = []

    def chip(d):
        return lax.rem(x + d, 4)

    def along_x(d):
        return (2 * chip(d) + c, ex)

    def along_y(d):
        return (me, lax.rem(y + d, 4) * 4 + z)

    def along_z(d):
        return (me, y * 4 + lax.rem(z + d, 4))

    def in_row(d):
        return (lax.rem(me + d, NSEQ), ex)

    def block(s):
        return pl.ds(pl.multiple_of(s * TOK, TOK), TOK)

    def cached(s):
        return pl.ds(pl.multiple_of(s * CDEV, CDEV), CDEV)

    def fresh(s):
        return pl.ds(pl.multiple_of(NSEQ * CDEV + s * TOK, TOK), TOK)

    def head(h):
        return pl.ds(pl.multiple_of(h * HD, HD), HD)

    def span(k):
        return pl.ds(k * CHUNK, CHUNK)

    def send(src, dst, sends, recvs, to):
        cp = pltpu.make_async_remote_copy(
            src_ref=src, dst_ref=dst, send_sem=sends, recv_sem=recvs,
            device_id=to, device_id_type=MESH,
        )
        cp.start()
        everything.append(cp)
        return cp

    def fetch(i, src, dst):
        cp = pltpu.make_async_copy(src, dst, loc_sem.at[i])
        cp.start()
        return cp

    barrier = pltpu.get_barrier_semaphore()
    for d in range(1, NSEQ):
        pl.semaphore_signal(barrier, inc=1, device_id=in_row(d), device_id_type=MESH)
    for d in range(1, 4):
        pl.semaphore_signal(barrier, inc=1, device_id=along_y(d), device_id_type=MESH)
        pl.semaphore_signal(barrier, inc=1, device_id=along_z(d), device_id_type=MESH)

    lanes = pl.ds(0, HD)
    own_q = fetch(0, q_hbm.at[:, pl.ds(pl.multiple_of(me * 512, 512), 512)], qbuf.at[block(me), :])
    own_kn = fetch(1, kn_hbm.at[:, head(x)], kbuf.at[fresh(me), lanes])
    own_vn = fetch(2, vn_hbm.at[:, head(x)], vbuf.at[fresh(me), lanes])
    own_k = fetch(3, kc_hbm.at[:, head(x)], kbuf.at[cached(me), lanes])
    own_v = fetch(4, vc_hbm.at[:, head(x)], vbuf.at[cached(me), lanes])

    lane = lax.broadcasted_iota(jnp.int32, (TOK, EXPERTS), 1)
    chosen = jnp.zeros((TOK, EXPERTS), f32)
    for k in range(TOPK):
        chosen = chosen + jnp.where(ids_ref[:, k:k + 1] == lane, f32(1.0), f32(0.0))
    before = (lax.broadcasted_iota(jnp.int32, (TOK, TOK), 1)
              < lax.broadcasted_iota(jnp.int32, (TOK, TOK), 0)).astype(f32)
    rank = jnp.dot(before.astype(bf), chosen.astype(bf), preferred_element_type=f32)
    first = (CAP * me + 1).astype(f32)
    table[block(me), :] = jnp.where(chosen > 0, rank + first, f32(0.0)).astype(bf)

    pl.semaphore_wait(barrier, NSEQ - 1 + 6)
    q_copies, n_copies, c_copies = [], [], []
    for d in (4, 2, 6, 3, 5, 1, 7):
        to = lax.rem(me + d, NSEQ)
        q_copies.append(send(
            q_hbm.at[:, pl.ds(pl.multiple_of(to * 512, 512), 512)], qbuf.at[block(me), :],
            q_send.at[d], q_recv.at[d], in_row(d)))
    for d in (4, 2, 6, 3, 5, 1, 7):
        h = lax.rem(me + d, NSEQ) // 2
        for i, (src, dst) in enumerate(((kn_hbm, kbuf), (vn_hbm, vbuf))):
            n_copies.append(send(
                src.at[:, head(h)], dst.at[fresh(me), lanes],
                n_send.at[d, i], n_recv.at[d, i], in_row(d)))
    fw_copies = {0: [
        send(src.at[:, head(x)], dst.at[cached(me), lanes],
             fw_send.at[0, i], fw_recv.at[0, i], sibling)
        for i, (src, dst) in enumerate(((kc_hbm, kbuf), (vc_hbm, vbuf)))
    ]}
    kv_copies = {}
    for d in (1, 3, 2):
        kv_copies[d] = [
            send(src.at[:, head(chip(d))], dst.at[cached(me), lanes],
                 kv_send.at[d, i], kv_recv.at[d, i], along_x(d))
            for i, (src, dst) in enumerate(((kc_hbm, kbuf), (vc_hbm, vbuf)))
        ]
    for d in range(1, NSEQ):
        view = table.at[block(me), :]
        c_copies.append(send(view, view, c_send.at[d], c_recv.at[d], in_row(d)))
    get_w = fetch(5, w_hbm, wbuf)
    get_res = fetch(6, res_hbm, resbuf)
    get_router = fetch(7, router_hbm, router)
    get_wg = fetch(8, wg_hbm, wg)
    get_wu = fetch(9, wu_hbm, wu)
    get_wd = fetch(10, wd_hbm, wd)

    total = NSEQ * (CDEV + TOK)
    lane = lax.broadcasted_iota(jnp.int32, (total, HD), 1)
    pos = lax.broadcasted_iota(jnp.int32, (total, HD), 0)
    hidden = (pos >= len_ref[0]) & (pos < NSEQ * CDEV) & (lane == 0)
    kbuf[:, HD:] = jnp.where(hidden, f32(-1e30), f32(0.0)).astype(bf)
    vbuf[:, HD:] = jnp.ones((total, HD), bf)
    acc[...] = jnp.zeros_like(acc)
    mbuf[...] = jnp.full(mbuf.shape, -3e38, f32)
    unit = (lax.broadcasted_iota(jnp.int32, (DOCTOK, HD), 1) == 0).astype(f32).astype(bf)
    for h in range(4):
        qext[h, :, HD:] = unit

    for cp in q_copies:
        cp.wait_recv()
    own_q.wait()
    for h in range(4):
        qext[h, :, :HD] = qbuf[:, h * HD:(h + 1) * HD]

    factor = f32(LOG2E / (HD ** 0.5))

    def attend(begin, count, causal):
        keys_at = pl.ds(begin, count)

        def one_head(h, carry):
            for half in range(2):
                rows = pl.ds(half * 256, 256)
                s = lax.dot_general(
                    qext[h, rows, :], kbuf[keys_at, :], NT, preferred_element_type=f32
                )
                if causal:
                    t = lax.broadcasted_iota(jnp.int32, s.shape, 0) + half * 256
                    u = lax.broadcasted_iota(jnp.int32, s.shape, 1)
                    s = jnp.where(u <= t, s, f32(-1e30))
                m_old = mbuf[h, rows, :]
                m_new = jnp.maximum(m_old, jnp.max(s, axis=1, keepdims=True))
                mbuf[h, rows, :] = m_new
                alpha = jnp.exp2((m_old - m_new) * factor)
                p = jnp.exp2((s - m_new[:, :1]) * factor).astype(bf)
                pv = jnp.dot(p, vbuf[keys_at, :], preferred_element_type=f32)
                acc[h, rows, :HD] = acc[h, rows, :HD] * alpha + pv[:, :HD]
                acc[h, rows, HD:] = acc[h, rows, HD:] * alpha + pv[:, HD:]
            return carry

        lax.fori_loop(0, 4, one_head, 0)

    def forward_kv(d):
        for cp in kv_copies[d]:
            cp.wait_recv()
        src = 2 * lax.rem(x + 4 - d, 4) + c
        fw_copies[d] = [
            send(view, view, fw_send.at[d, i], fw_recv.at[d, i], sibling)
            for i, view in enumerate((kbuf.at[cached(src), lanes], vbuf.at[cached(src), lanes]))
        ]

    def attend_chip(d):
        for cp in fw_copies[d]:
            cp.wait_recv()
        attend(pl.multiple_of(lax.rem(x + 4 - d, 4) * 1024, 1024), 1024, False)

    own_k.wait()
    own_v.wait()
    attend_chip(0)
    own_kn.wait()
    own_vn.wait()
    for cp in n_copies:
        cp.wait_recv()
    attend(NSEQ * CDEV, DOCTOK, True)
    forward_kv(1)
    forward_kv(3)

    qi = lax.broadcasted_iota(jnp.int32, (ROWS, EXPERTS), 0)
    ei = (lax.broadcasted_iota(jnp.int32, (ROWS, EXPERTS), 1) - me * PEERS) * SLOTS
    owner = jnp.where((qi >= ei) & (qi < ei + SLOTS), f32(1.0), f32(0.0)).astype(bf)

    def within(shape, axis):
        at = lax.broadcasted_iota(jnp.int32, shape, axis)
        low = at + 1
        for e in range(1, PEERS):
            low = jnp.where(at >= e * SLOTS, at + 1 - e * SLOTS, low)
        return low.astype(f32)

    for cp in c_copies:
        cp.wait_recv()
    by_row = lax.dot_general(owner, table[...], NT, preferred_element_type=f32)
    pick[...] = jnp.where(by_row == within((ROWS, 128), 0)[:, :1], f32(1.0), f32(0.0)).astype(bf)

    attend_chip(1)
    forward_kv(2)
    attend_chip(3)
    attend_chip(2)

    get_w.wait()
    get_res.wait()
    get_router.wait()
    for d in range(4):
        for i, core in enumerate((other, c)):
            at = block(2 * chip(d) + core)
            for h in range(4):
                attn[i, d, :, h * HD:(h + 1) * HD] = (
                    acc[h, at, :HD] / acc[h, at, HD:]
                ).astype(bf)

    s_copies, x_copies = {}, {}

    def sum_cores(k):
        sib_out[:, :, span(k)] = jnp.dot(
            attn[0].reshape(4 * TOK, 512), wbuf[:, span(k)], preferred_element_type=f32
        ).astype(bf).reshape(4, TOK, CHUNK)
        view = sib_out.at[:, :, span(k)]
        s_copies[k] = send(view, sib_in.at[:, :, span(k)], s_send.at[k], s_recv.at[k], sibling)
        part[:, :, span(k)] = jnp.dot(
            attn[1].reshape(4 * TOK, 512), wbuf[:, span(k)], preferred_element_type=f32
        ).reshape(4, TOK, CHUNK)

    def sum_chips(k):
        s_copies[k].wait_recv()
        x_copies[k] = []
        for d in (2, 1, 3):
            x_out[d, :, span(k)] = (
                part[d, :, span(k)] + sib_in[d, :, span(k)].astype(f32)
            ).astype(bf)
            x_copies[k].append(send(
                x_out.at[d, :, span(k)], x_in.at[d, :, span(k)],
                x_send.at[k, d], x_recv.at[k, d], along_x(d)))

    a_copies, f_copies = {}, {}

    def spread(k):
        mine = (resbuf[:, span(k)].astype(f32) + part[0, :, span(k)]
                + sib_in[0, :, span(k)].astype(f32))
        for cp in x_copies[k]:
            cp.wait_recv()
        for d in (1, 2, 3):
            mine = mine + x_in[d, :, span(k)].astype(f32)
        mixed[:, span(k)] = mine
        tokens[block(me), span(k)] = (mine * gain_ref[:, span(k)]).astype(bf)
        view = tokens.at[block(me), span(k)]
        a_copies[k] = {
            d: send(view, view, a_send.at[k, d], a_recv.at[k, d],
                    sibling if d == 0 else along_x(d))
            for d in (2, 1, 3, 0)
        }

    def forward(k):
        f_copies[k] = []
        for d in (1, 3, 2):
            a_copies[k][d].wait_recv()
            view = tokens.at[block(2 * lax.rem(x + 4 - d, 4) + c), span(k)]
            f_copies[k].append(send(view, view, f_send.at[k, d], f_recv.at[k, d], sibling))

    def hop(even, at, source, target, sends, recvs, base):
        copies = []
        for d in (1, 3, 2):
            if even:
                src, dst, to = source.at[lax.rem(y + d, 4), :, :, at], target.at[y, :, :, at], along_y(d)
            else:
                src, dst, to = source.at[:, lax.rem(z + d, 4), :, at], target.at[:, z, :, at], along_z(d)
            copies.append(send(src, dst, sends.at[base + d], recvs.at[base + d], to))
        if even:
            target[y, :, :, at] = source[y, :, :, at]
        else:
            target[:, z, :, at] = source[:, z, :, at]
        return copies

    d_first, d_second, r_first, r_second = {}, {}, {}, {}

    def dispatch(k):
        a_copies[k][0].wait_recv()
        for cp in f_copies[k]:
            cp.wait_recv()
        outbox[:, :, :, span(k)] = jnp.dot(
            pick[...], tokens[:, span(k)], preferred_element_type=f32
        ).astype(bf).reshape(4, 4, SLOTS, CHUNK)
        d_first[k] = hop(k % 2 == 0, span(k), outbox, relay_out, d_send, d_recv, 8 * k)

    def dispatch_on(k):
        for cp in d_first[k]:
            cp.wait_recv()
        d_second[k] = hop(k % 2 == 1, span(k), relay_out, inbox, d_send, d_recv, 8 * k + 4)

    stages = (sum_cores, sum_chips, spread, forward, dispatch)
    for t in range(NCHUNK + len(stages) - 1):
        for i, stage in enumerate(stages):
            if 0 <= t - i < NCHUNK:
                stage(t - i)
        if t == NCHUNK + 1:
            mx = mixed[...]
            factor_of = f32(1.0) / jnp.sqrt(jnp.mean(mx * mx, axis=1, keepdims=True) + 1e-06)
            normed = (mx * factor_of * gain_ref[...]).astype(bf)
            logits = jnp.dot(normed, router[...], preferred_element_type=f32)
            expo = jnp.where(chosen > 0, jnp.exp(logits), f32(0.0))
            gtable[block(me), :EXPERTS] = expo / jnp.sum(expo, axis=1, keepdims=True)
            gtable[block(me), EXPERTS:] = jnp.broadcast_to(factor_of, (TOK, EXPERTS))
            view = gtable.at[block(me), :]
            g_copies = [
                send(view, view, g_send.at[d], g_recv.at[d], in_row(d)) for d in range(1, NSEQ)
            ]
        if t == NCHUNK + 2:
            dispatch_on(0)

    for cp in g_copies:
        cp.wait_recv()
    fac = gtable[:, EXPERTS:]
    high = fac.astype(bf)
    rest = fac - high.astype(f32)
    mid = rest.astype(bf)
    low = (rest - mid.astype(f32)).astype(bf)
    by_slot = (jnp.dot(pick[...], high, preferred_element_type=f32)
               + jnp.dot(pick[...], mid, preferred_element_type=f32)
               + jnp.dot(pick[...], low, preferred_element_type=f32))
    slot_lane = lax.broadcasted_iota(jnp.int32, (PEERS, SLOTS, 128), 2)
    slot_row = lax.broadcasted_iota(jnp.int32, (PEERS, SLOTS, 128), 1)
    lined = jnp.sum(
        jnp.where(slot_lane == slot_row, by_slot.reshape(PEERS, SLOTS, 128), f32(0.0)), axis=1
    )
    rbox[...] = jnp.broadcast_to(lined[:, None, :], (PEERS, 8, 128)).reshape(4, 4, 8, 128)
    every = pl.ds(0, 128)
    rf = hop(True, every, rbox, rrelay, d_send, d_recv, 8 * NCHUNK)

    dispatch_on(1)
    dispatch_on(2)
    dispatch_on(3)
    for cp in rf:
        cp.wait_recv()
    rs = hop(False, every, rrelay, rin, d_send, d_recv, 8 * NCHUNK + 4)

    by_token = lax.dot_general(table[...], owner, NT, preferred_element_type=f32)
    share = lax.dot_general(gtable[:, :EXPERTS].astype(bf), owner, NT, preferred_element_type=f32)
    give[...] = jnp.where(by_token == within((8, ROWS), 1)[:1, :], share, f32(0.0)).astype(bf)

    get_wg.wait()
    get_wu.wait()
    for k in range(NCHUNK):
        for cp in d_second[k]:
            cp.wait_recv()
        rows = inbox[:, :, :, span(k)].reshape(ROWS, CHUNK)
        g = jnp.dot(rows, wg[span(k), :], preferred_element_type=f32)
        u = jnp.dot(rows, wu[span(k), :], preferred_element_type=f32)
        if k == 0:
            hg[...] = g
            hu[...] = u
        else:
            hg[...] += g
            hu[...] += u
    for cp in rs:
        cp.wait_recv()
    got = rin[...].reshape(PEERS, 8, 128)[:, :1, :]
    scale = jnp.sum(jnp.where(slot_lane == slot_row, got, f32(0.0)), axis=2, keepdims=True)
    scale = scale.reshape(ROWS, 1)
    g = hg[...] * scale
    act[...] = (g / (f32(1.0) + jnp.exp(-g)) * (hu[...] * scale)).astype(bf)
    get_wd.wait()
    reused = [cp for k in range(NCHUNK) for cp in d_first[k] + x_copies[k] + [s_copies[k]]]
    for cp in reused:
        cp.wait_send()
    for k in range(NCHUNK):
        outbox[:, :, :, span(k)] = jnp.dot(
            act[...], wd[:, span(k)], preferred_element_type=f32
        ).astype(bf).reshape(4, 4, SLOTS, CHUNK)
        r_first[k] = hop(k % 2 == 0, span(k), outbox, relay_back, r_send, r_recv, 8 * k)

    for k in range(NCHUNK):
        for cp in r_first[k]:
            cp.wait_recv()
        r_second[k] = hop(k % 2 == 1, span(k), relay_back, back, r_send, r_recv, 8 * k + 4)

    s2_copies, x2_copies = {}, {}

    def combine(k):
        for cp in r_second[k]:
            cp.wait_recv()
        returned = back[:, :, :, span(k)].reshape(ROWS, CHUNK)
        for d in (2, 1, 3, 0):
            sib_out[d, :, span(k)] = jnp.dot(
                give[block(2 * chip(d) + other), :], returned, preferred_element_type=f32
            ).astype(bf)
        view = sib_out.at[:, :, span(k)]
        s2_copies[k] = send(view, sib_in2.at[:, :, span(k)], s2_send.at[k], s2_recv.at[k], sibling)
        for d in (2, 1, 3, 0):
            part[d, :, span(k)] = jnp.dot(
                give[block(2 * chip(d) + c), :], returned, preferred_element_type=f32
            )

    def combine_chips(k):
        s2_copies[k].wait_recv()
        x2_copies[k] = []
        for d in (2, 1, 3):
            x_out[d, :, span(k)] = (
                part[d, :, span(k)] + sib_in2[d, :, span(k)].astype(f32)
            ).astype(bf)
            x2_copies[k].append(send(
                x_out.at[d, :, span(k)], x_in2.at[d, :, span(k)],
                x2_send.at[k, d], x2_recv.at[k, d], along_x(d)))

    for k in range(NCHUNK):
        combine(k)
        if k:
            combine_chips(k - 1)
    combine_chips(NCHUNK - 1)
    for k in range(NCHUNK):
        out = mixed[:, span(k)] + part[0, :, span(k)] + sib_in2[0, :, span(k)].astype(f32)
        for cp in x2_copies[k]:
            cp.wait_recv()
        for d in (1, 2, 3):
            out = out + x_in2[d, :, span(k)].astype(f32)
        out_ref[:, span(k)] = out.astype(bf)

    for cp in everything:
        if not any(cp is done for done in reused):
            cp.wait_send()


def layer(
    queries, new_keys, new_values, cache_keys, cache_values, cache_len, residual_in,
    out_weight, norm_gain, router_weight, expert_ids, gate_proj, up_proj, down_proj,
):
    hbm = pl.BlockSpec(memory_space=pl.ANY)
    vmem = pl.BlockSpec(memory_space=pltpu.VMEM)
    bf, f32 = jnp.bfloat16, jnp.float32
    dma = pltpu.SemaphoreType.DMA
    total = NSEQ * (CDEV + TOK)
    plane = pltpu.VMEM((4, 4, SLOTS, WIDTH), bf)
    small = pltpu.VMEM((4, 4, 8, 128), f32)
    row = pltpu.VMEM((4, TOK, WIDTH), bf)
    out = pl.pallas_call(
        layer_kernel,
        out_shape=jax.ShapeDtypeStruct((TOK, WIDTH), bf),
        in_specs=[pl.BlockSpec(memory_space=pltpu.SMEM), vmem, vmem] + [hbm] * 11,
        out_specs=vmem,
        scratch_shapes=[
            pltpu.VMEM((DOCTOK, 512), bf),
            pltpu.VMEM((4, DOCTOK, 256), bf),
            pltpu.VMEM((total, 256), bf),
            pltpu.VMEM((total, 256), bf),
            pltpu.VMEM((4, DOCTOK, 256), f32),
            pltpu.VMEM((4, DOCTOK, HD), f32),
            pltpu.VMEM((2, 4, TOK, 512), bf),
            pltpu.VMEM((512, WIDTH), bf),
            pltpu.VMEM((TOK, WIDTH), bf),
            pltpu.VMEM((WIDTH, EXPERTS), bf),
            pltpu.VMEM((4, TOK, WIDTH), f32),
            row, row, row, row, row, row,
            pltpu.VMEM((TOK, WIDTH), f32),
            pltpu.VMEM((DOCTOK, WIDTH), bf),
            pltpu.VMEM((DOCTOK, EXPERTS), bf),
            pltpu.VMEM((DOCTOK, 2 * EXPERTS), f32),
            pltpu.VMEM((ROWS, DOCTOK), bf),
            pltpu.VMEM((DOCTOK, ROWS), bf),
            plane, plane, plane, plane, plane,
            small, small, small,
            pltpu.VMEM((WIDTH, FF), bf),
            pltpu.VMEM((WIDTH, FF), bf),
            pltpu.VMEM((FF, WIDTH), bf),
            pltpu.VMEM((ROWS, FF), f32),
            pltpu.VMEM((ROWS, FF), f32),
            pltpu.VMEM((ROWS, FF), bf),
            dma((11,)), dma((8,)), dma((8,)), dma((8,)), dma((8,)), dma((8, 2)), dma((8, 2)),
            dma((4, 2)), dma((4, 2)), dma((4, 2)), dma((4, 2)),
            dma((NCHUNK,)), dma((NCHUNK,)), dma((NCHUNK, 4)), dma((NCHUNK, 4)),
            dma((NCHUNK, 4)), dma((NCHUNK, 4)), dma((NCHUNK, 4)), dma((NCHUNK, 4)),
            dma((8,)), dma((8,)),
            dma((8 * NCHUNK + 8,)), dma((8 * NCHUNK + 8,)), dma((8 * NCHUNK,)), dma((8 * NCHUNK,)),
            dma((NCHUNK,)), dma((NCHUNK,)), dma((NCHUNK, 4)), dma((NCHUNK, 4)),
        ],
        compiler_params=pltpu.CompilerParams(
            collective_id=0, has_side_effects=True, vmem_limit_bytes=67043328
        ),
        name="whole_layer",
    )(cache_len, expert_ids[0], norm_gain.reshape(1, WIDTH), queries[0], new_keys[0],
      new_values[0], cache_keys[0], cache_values[0], out_weight, residual_in[0],
      router_weight, gate_proj[0], up_proj[0], down_proj[0])
    return out.reshape(1, TOK, WIDTH)


def solution(mesh):
    in_specs = (
        P("exp", "seq", None),
        P("exp", "seq", None),
        P("exp", "seq", None),
        P("exp", "seq", None),
        P("exp", "seq", None),
        P("exp"),
        P("exp", "seq", None),
        P("seq", None),
        P(),
        P(),
        P("exp", "seq", None),
        P(("seq", "exp"), None, None),
        P(("seq", "exp"), None, None),
        P(("seq", "exp"), None, None),
    )
    out_specs = P("exp", "seq", None)
    return jax.shard_map(layer, mesh=mesh, in_specs=in_specs, out_specs=out_specs, check_vma=False)
```

```python
import jax
import jax.numpy as jnp
from jax import lax
from jax.experimental import pallas as pl
from jax.experimental.pallas import tpu as pltpu
from jax.sharding import PartitionSpec as P

QH = 32
KVH = 4
HD = 128
TOPK = 8
NSEQ = 8
TOK = 64
DOCTOK = 512
CDEV = 512
WIDTH = 2048
LOG2E = 1.4426950408889634
MESH = pl.DeviceIdType.MESH


EXPERTS = 128
FF = 768
PEERS = 16
SLOTS = 48
CAP = 6
ROWS = PEERS * SLOTS
NCHUNK = 4
CHUNK = WIDTH // NCHUNK
AHEAD = 6
NT = (((1,), (1,)), ((), ()))


def layer_kernel(
    len_ref, ids_ref, gain_ref, q_hbm, kn_hbm, vn_hbm, kc_hbm, vc_hbm, w_hbm, res_hbm,
    router_hbm, wg_hbm, wu_hbm, wd_hbm, out_ref,
    qbuf, qext, kbuf, vbuf, acc, mbuf, attn, wbuf, resbuf, router, part,
    sib_out, sib_in, x_out, x_in, sib_in2, x_in2,
    mixed, tokens, table, gtable, pick, give, outbox, relay_out, inbox, relay_back, back,
    rbox, rrelay, rin, wg, wu, wd, hg, hu, act,
    loc_sem, c_send, c_recv, q_send, q_recv, n_send, n_recv, kv_send, kv_recv, fw_send, fw_recv,
    s_send, s_recv, x_send, x_recv, a_send, a_recv, f_send, f_recv, g_send, g_recv,
    d_send, d_recv, r_send, r_recv, s2_send, s2_recv, x2_send, x2_recv,
):
    me = lax.axis_index("seq")
    ex = lax.axis_index("exp")
    x, c = me // 2, lax.rem(me, 2)
    y, z = ex // 4, lax.rem(ex, 4)
    other = 1 - c
    sibling = (2 * x + other, ex)
    f32, bf = jnp.float32, jnp.bfloat16
    everything = []

    def chip(d):
        return lax.rem(x + d, 4)

    def along_x(d):
        return (2 * chip(d) + c, ex)

    def along_y(d):
        return (me, lax.rem(y + d, 4) * 4 + z)

    def along_z(d):
        return (me, y * 4 + lax.rem(z + d, 4))

    def in_row(d):
        return (lax.rem(me + d, NSEQ), ex)

    def block(s):
        return pl.ds(pl.multiple_of(s * TOK, TOK), TOK)

    def cached(s):
        return pl.ds(pl.multiple_of(s * CDEV, CDEV), CDEV)

    def fresh(s):
        return pl.ds(pl.multiple_of(NSEQ * CDEV + s * TOK, TOK), TOK)

    def head(h):
        return pl.ds(pl.multiple_of(h * HD, HD), HD)

    def span(k):
        return pl.ds(k * CHUNK, CHUNK)

    def send(src, dst, sends, recvs, to):
        cp = pltpu.make_async_remote_copy(
            src_ref=src, dst_ref=dst, send_sem=sends, recv_sem=recvs,
            device_id=to, device_id_type=MESH,
        )
        cp.start()
        everything.append(cp)
        return cp

    def fetch(i, src, dst):
        cp = pltpu.make_async_copy(src, dst, loc_sem.at[i])
        cp.start()
        return cp

    barrier = pltpu.get_barrier_semaphore()
    for d in range(1, NSEQ):
        pl.semaphore_signal(barrier, inc=1, device_id=in_row(d), device_id_type=MESH)
    for d in range(1, 4):
        pl.semaphore_signal(barrier, inc=1, device_id=along_y(d), device_id_type=MESH)
        pl.semaphore_signal(barrier, inc=1, device_id=along_z(d), device_id_type=MESH)

    lanes = pl.ds(0, HD)
    own_q = fetch(0, q_hbm.at[:, pl.ds(pl.multiple_of(me * 512, 512), 512)], qbuf.at[block(me), :])
    own_kn = fetch(1, kn_hbm.at[:, head(x)], kbuf.at[fresh(me), lanes])
    own_vn = fetch(2, vn_hbm.at[:, head(x)], vbuf.at[fresh(me), lanes])
    own_k = fetch(3, kc_hbm.at[:, head(x)], kbuf.at[cached(me), lanes])
    own_v = fetch(4, vc_hbm.at[:, head(x)], vbuf.at[cached(me), lanes])

    lane = lax.broadcasted_iota(jnp.int32, (TOK, EXPERTS), 1)
    chosen = jnp.zeros((TOK, EXPERTS), f32)
    for k in range(TOPK):
        chosen = chosen + jnp.where(ids_ref[:, k:k + 1] == lane, f32(1.0), f32(0.0))
    before = (lax.broadcasted_iota(jnp.int32, (TOK, TOK), 1)
              < lax.broadcasted_iota(jnp.int32, (TOK, TOK), 0)).astype(f32)
    rank = jnp.dot(before.astype(bf), chosen.astype(bf), preferred_element_type=f32)
    first = (CAP * me + 1).astype(f32)
    table[block(me), :] = jnp.where(chosen > 0, rank + first, f32(0.0)).astype(bf)

    pl.semaphore_wait(barrier, NSEQ - 1 + 6)
    q_copies, n_copies, c_copies = [], [], []
    for d in (4, 2, 6, 3, 5, 1, 7):
        to = lax.rem(me + d, NSEQ)
        q_copies.append(send(
            q_hbm.at[:, pl.ds(pl.multiple_of(to * 512, 512), 512)], qbuf.at[block(me), :],
            q_send.at[d], q_recv.at[d], in_row(d)))
    for d in (4, 2, 6, 3, 5, 1, 7):
        h = lax.rem(me + d, NSEQ) // 2
        for i, (src, dst) in enumerate(((kn_hbm, kbuf), (vn_hbm, vbuf))):
            n_copies.append(send(
                src.at[:, head(h)], dst.at[fresh(me), lanes],
                n_send.at[d, i], n_recv.at[d, i], in_row(d)))
    fw_copies = {0: [
        send(src.at[:, head(x)], dst.at[cached(me), lanes],
             fw_send.at[0, i], fw_recv.at[0, i], sibling)
        for i, (src, dst) in enumerate(((kc_hbm, kbuf), (vc_hbm, vbuf)))
    ]}
    kv_copies = {}
    for d in (1, 3, 2):
        kv_copies[d] = [
            send(src.at[:, head(chip(d))], dst.at[cached(me), lanes],
                 kv_send.at[d, i], kv_recv.at[d, i], along_x(d))
            for i, (src, dst) in enumerate(((kc_hbm, kbuf), (vc_hbm, vbuf)))
        ]
    for d in range(1, NSEQ):
        view = table.at[block(me), :]
        c_copies.append(send(view, view, c_send.at[d], c_recv.at[d], in_row(d)))
    get_w = fetch(5, w_hbm, wbuf)
    get_res = fetch(6, res_hbm, resbuf)
    get_router = fetch(7, router_hbm, router)
    get_wg = fetch(8, wg_hbm, wg)
    get_wu = fetch(9, wu_hbm, wu)
    get_wd = fetch(10, wd_hbm, wd)

    total = NSEQ * (CDEV + TOK)
    lane = lax.broadcasted_iota(jnp.int32, (total, HD), 1)
    pos = lax.broadcasted_iota(jnp.int32, (total, HD), 0)
    hidden = (pos >= len_ref[0]) & (pos < NSEQ * CDEV) & (lane == 0)
    kbuf[:, HD:] = jnp.where(hidden, f32(-1e30), f32(0.0)).astype(bf)
    vbuf[:, HD:] = jnp.ones((total, HD), bf)
    acc[...] = jnp.zeros_like(acc)
    mbuf[...] = jnp.full(mbuf.shape, -3e38, f32)
    unit = (lax.broadcasted_iota(jnp.int32, (DOCTOK, HD), 1) == 0).astype(f32).astype(bf)
    for h in range(4):
        qext[h, :, HD:] = unit

    for cp in q_copies:
        cp.wait_recv()
    own_q.wait()
    for h in range(4):
        qext[h, :, :HD] = qbuf[:, h * HD:(h + 1) * HD]

    factor = f32(LOG2E / (HD ** 0.5))

    def attend(begin, count, causal):
        keys_at = pl.ds(begin, count)

        def heads_of(i, carry):
            tiles = [(i * 2 + j, r * 256) for j in range(2) for r in range(2)]
            scores = []
            for h, r in tiles:
                s = lax.dot_general(
                    qext[h, pl.ds(r, 256), :], kbuf[keys_at, :], NT, preferred_element_type=f32
                )
                if causal:
                    t = lax.broadcasted_iota(jnp.int32, s.shape, 0) + r
                    u = lax.broadcasted_iota(jnp.int32, s.shape, 1)
                    s = jnp.where(u <= t, s, f32(-1e30))
                scores.append(s)
            for (h, r), s in zip(tiles, scores):
                rows = pl.ds(r, 256)
                m_old = mbuf[h, rows, :]
                m_new = jnp.maximum(m_old, jnp.max(s, axis=1, keepdims=True))
                mbuf[h, rows, :] = m_new
                alpha = jnp.exp2((m_old - m_new) * factor)
                p = jnp.exp2((s - m_new[:, :1]) * factor).astype(bf)
                pv = jnp.dot(p, vbuf[keys_at, :], preferred_element_type=f32)
                acc[h, rows, :HD] = acc[h, rows, :HD] * alpha + pv[:, :HD]
                acc[h, rows, HD:] = acc[h, rows, HD:] * alpha + pv[:, HD:]
            return carry

        lax.fori_loop(0, 2, heads_of, 0)

    def forward_kv(d):
        for cp in kv_copies[d]:
            cp.wait_recv()
        src = 2 * lax.rem(x + 4 - d, 4) + c
        fw_copies[d] = [
            send(view, view, fw_send.at[d, i], fw_recv.at[d, i], sibling)
            for i, view in enumerate((kbuf.at[cached(src), lanes], vbuf.at[cached(src), lanes]))
        ]

    def attend_chip(d):
        for cp in fw_copies[d]:
            cp.wait_recv()
        attend(pl.multiple_of(lax.rem(x + 4 - d, 4) * 1024, 1024), 1024, False)

    own_k.wait()
    own_v.wait()
    attend_chip(0)
    own_kn.wait()
    own_vn.wait()
    for cp in n_copies:
        cp.wait_recv()
    attend(NSEQ * CDEV, DOCTOK, True)
    forward_kv(1)
    forward_kv(3)

    qi = lax.broadcasted_iota(jnp.int32, (ROWS, EXPERTS), 0)
    ei = (lax.broadcasted_iota(jnp.int32, (ROWS, EXPERTS), 1) - me * PEERS) * SLOTS
    owner = jnp.where((qi >= ei) & (qi < ei + SLOTS), f32(1.0), f32(0.0)).astype(bf)

    def within(shape, axis):
        at = lax.broadcasted_iota(jnp.int32, shape, axis)
        low = at + 1
        for e in range(1, PEERS):
            low = jnp.where(at >= e * SLOTS, at + 1 - e * SLOTS, low)
        return low.astype(f32)

    for cp in c_copies:
        cp.wait_recv()
    by_row = lax.dot_general(owner, table[...], NT, preferred_element_type=f32)
    pick[...] = jnp.where(by_row == within((ROWS, 128), 0)[:, :1], f32(1.0), f32(0.0)).astype(bf)

    attend_chip(1)
    forward_kv(2)
    attend_chip(3)
    attend_chip(2)

    get_w.wait()
    get_res.wait()
    get_router.wait()
    for d in range(4):
        for i, core in enumerate((other, c)):
            at = block(2 * chip(d) + core)
            for h in range(4):
                attn[i, d, :, h * HD:(h + 1) * HD] = (
                    acc[h, at, :HD] / acc[h, at, HD:]
                ).astype(bf)

    s_copies, x_copies = {}, {}

    def sum_cores(k):
        sib_out[:, :, span(k)] = jnp.dot(
            attn[0].reshape(4 * TOK, 512), wbuf[:, span(k)], preferred_element_type=f32
        ).astype(bf).reshape(4, TOK, CHUNK)
        view = sib_out.at[:, :, span(k)]
        s_copies[k] = send(view, sib_in.at[:, :, span(k)], s_send.at[k], s_recv.at[k], sibling)
        part[:, :, span(k)] = jnp.dot(
            attn[1].reshape(4 * TOK, 512), wbuf[:, span(k)], preferred_element_type=f32
        ).reshape(4, TOK, CHUNK)

    def sum_chips(k):
        s_copies[k].wait_recv()
        x_copies[k] = []
        for d in (2, 1, 3):
            x_out[d, :, span(k)] = (
                part[d, :, span(k)] + sib_in[d, :, span(k)].astype(f32)
            ).astype(bf)
            x_copies[k].append(send(
                x_out.at[d, :, span(k)], x_in.at[d, :, span(k)],
                x_send.at[k, d], x_recv.at[k, d], along_x(d)))

    a_copies, f_copies = {}, {}

    def spread(k):
        mine = (resbuf[:, span(k)].astype(f32) + part[0, :, span(k)]
                + sib_in[0, :, span(k)].astype(f32))
        for cp in x_copies[k]:
            cp.wait_recv()
        for d in (1, 2, 3):
            mine = mine + x_in[d, :, span(k)].astype(f32)
        mixed[:, span(k)] = mine
        tokens[block(me), span(k)] = (mine * gain_ref[:, span(k)]).astype(bf)
        view = tokens.at[block(me), span(k)]
        a_copies[k] = {
            d: send(view, view, a_send.at[k, d], a_recv.at[k, d],
                    sibling if d == 0 else along_x(d))
            for d in (2, 1, 3, 0)
        }

    def forward(k):
        f_copies[k] = []
        for d in (1, 3, 2):
            a_copies[k][d].wait_recv()
            view = tokens.at[block(2 * lax.rem(x + 4 - d, 4) + c), span(k)]
            f_copies[k].append(send(view, view, f_send.at[k, d], f_recv.at[k, d], sibling))

    def hop(even, at, source, target, sends, recvs, base):
        copies = []
        for d in (1, 3, 2):
            if even:
                src, dst, to = source.at[lax.rem(y + d, 4), :, :, at], target.at[y, :, :, at], along_y(d)
            else:
                src, dst, to = source.at[:, lax.rem(z + d, 4), :, at], target.at[:, z, :, at], along_z(d)
            copies.append(send(src, dst, sends.at[base + d], recvs.at[base + d], to))
        if even:
            target[y, :, :, at] = source[y, :, :, at]
        else:
            target[:, z, :, at] = source[:, z, :, at]
        return copies

    def both(k, turn, source, target, sends, recvs, base):
        copies = []
        for i in range(2):
            at = pl.ds(k * CHUNK + i * (CHUNK // 2), CHUNK // 2)
            copies += hop((i + turn) % 2 == 0, at, source, target, sends, recvs, base + 4 * i)
        return copies

    d_first, d_second, r_first, r_second = {}, {}, {}, {}

    def dispatch(k):
        a_copies[k][0].wait_recv()
        for cp in f_copies[k]:
            cp.wait_recv()
        outbox[:, :, :, span(k)] = jnp.dot(
            pick[...], tokens[:, span(k)], preferred_element_type=f32
        ).astype(bf).reshape(4, 4, SLOTS, CHUNK)
        d_first[k] = both(k, 0, outbox, relay_out, d_send, d_recv, 16 * k)

    def dispatch_on(k):
        for cp in d_first[k]:
            cp.wait_recv()
        d_second[k] = both(k, 1, relay_out, inbox, d_send, d_recv, 16 * k + 8)

    stages = (sum_cores, sum_chips, spread, forward, dispatch)
    for t in range(NCHUNK + len(stages) - 1):
        for i, stage in enumerate(stages):
            if 0 <= t - i < NCHUNK:
                stage(t - i)
        if t == NCHUNK + 1:
            mx = mixed[...]
            factor_of = f32(1.0) / jnp.sqrt(jnp.mean(mx * mx, axis=1, keepdims=True) + 1e-06)
            normed = (mx * factor_of * gain_ref[...]).astype(bf)
            logits = jnp.dot(normed, router[...], preferred_element_type=f32)
            expo = jnp.where(chosen > 0, jnp.exp(logits), f32(0.0))
            gtable[block(me), :EXPERTS] = expo / jnp.sum(expo, axis=1, keepdims=True)
            gtable[block(me), EXPERTS:] = jnp.broadcast_to(factor_of, (TOK, EXPERTS))
            view = gtable.at[block(me), :]
            g_copies = [
                send(view, view, g_send.at[d], g_recv.at[d], in_row(d)) for d in range(1, NSEQ)
            ]
        if t >= AHEAD:
            dispatch_on(t - AHEAD)

    for cp in g_copies:
        cp.wait_recv()
    fac = gtable[:, EXPERTS:]
    high = fac.astype(bf)
    rest = fac - high.astype(f32)
    mid = rest.astype(bf)
    low = (rest - mid.astype(f32)).astype(bf)
    by_slot = (jnp.dot(pick[...], high, preferred_element_type=f32)
               + jnp.dot(pick[...], mid, preferred_element_type=f32)
               + jnp.dot(pick[...], low, preferred_element_type=f32))
    slot_lane = lax.broadcasted_iota(jnp.int32, (PEERS, SLOTS, 128), 2)
    slot_row = lax.broadcasted_iota(jnp.int32, (PEERS, SLOTS, 128), 1)
    lined = jnp.sum(
        jnp.where(slot_lane == slot_row, by_slot.reshape(PEERS, SLOTS, 128), f32(0.0)), axis=1
    )
    rbox[...] = jnp.broadcast_to(lined[:, None, :], (PEERS, 8, 128)).reshape(4, 4, 8, 128)
    every = pl.ds(0, 128)
    rf = hop(True, every, rbox, rrelay, d_send, d_recv, 16 * NCHUNK)

    for k in range(NCHUNK + 4 - AHEAD, NCHUNK):
        dispatch_on(k)
    for cp in rf:
        cp.wait_recv()
    rs = hop(False, every, rrelay, rin, d_send, d_recv, 16 * NCHUNK + 4)

    by_token = lax.dot_general(table[...], owner, NT, preferred_element_type=f32)
    share = lax.dot_general(gtable[:, :EXPERTS].astype(bf), owner, NT, preferred_element_type=f32)
    give[...] = jnp.where(by_token == within((8, ROWS), 1)[:1, :], share, f32(0.0)).astype(bf)

    get_wg.wait()
    get_wu.wait()
    for k in range(NCHUNK):
        for cp in d_second[k]:
            cp.wait_recv()
        rows = inbox[:, :, :, span(k)].reshape(ROWS, CHUNK)
        g = jnp.dot(rows, wg[span(k), :], preferred_element_type=f32)
        u = jnp.dot(rows, wu[span(k), :], preferred_element_type=f32)
        if k == 0:
            hg[...] = g
            hu[...] = u
        else:
            hg[...] += g
            hu[...] += u
    for cp in rs:
        cp.wait_recv()
    got = rin[...].reshape(PEERS, 8, 128)[:, :1, :]
    scale = jnp.sum(jnp.where(slot_lane == slot_row, got, f32(0.0)), axis=2, keepdims=True)
    scale = scale.reshape(ROWS, 1)
    g = hg[...] * scale
    act[...] = (g / (f32(1.0) + jnp.exp(-g)) * (hu[...] * scale)).astype(bf)
    get_wd.wait()
    reused = [cp for k in range(NCHUNK) for cp in d_first[k] + x_copies[k] + [s_copies[k]]]
    for cp in reused:
        cp.wait_send()
    for k in range(NCHUNK):
        outbox[:, :, :, span(k)] = jnp.dot(
            act[...], wd[:, span(k)], preferred_element_type=f32
        ).astype(bf).reshape(4, 4, SLOTS, CHUNK)
        r_first[k] = both(k, 0, outbox, relay_back, r_send, r_recv, 16 * k)

    for k in range(NCHUNK):
        for cp in r_first[k]:
            cp.wait_recv()
        r_second[k] = both(k, 1, relay_back, back, r_send, r_recv, 16 * k + 8)

    s2_copies, x2_copies = {}, {}

    def combine(k):
        for cp in r_second[k]:
            cp.wait_recv()
        returned = back[:, :, :, span(k)].reshape(ROWS, CHUNK)
        for d in (2, 1, 3, 0):
            sib_out[d, :, span(k)] = jnp.dot(
                give[block(2 * chip(d) + other), :], returned, preferred_element_type=f32
            ).astype(bf)
        view = sib_out.at[:, :, span(k)]
        s2_copies[k] = send(view, sib_in2.at[:, :, span(k)], s2_send.at[k], s2_recv.at[k], sibling)
        for d in (2, 1, 3, 0):
            part[d, :, span(k)] = jnp.dot(
                give[block(2 * chip(d) + c), :], returned, preferred_element_type=f32
            )

    def combine_chips(k):
        s2_copies[k].wait_recv()
        x2_copies[k] = []
        for d in (2, 1, 3):
            x_out[d, :, span(k)] = (
                part[d, :, span(k)] + sib_in2[d, :, span(k)].astype(f32)
            ).astype(bf)
            x2_copies[k].append(send(
                x_out.at[d, :, span(k)], x_in2.at[d, :, span(k)],
                x2_send.at[k, d], x2_recv.at[k, d], along_x(d)))

    for k in range(NCHUNK):
        combine(k)
        if k:
            combine_chips(k - 1)
    combine_chips(NCHUNK - 1)
    for k in range(NCHUNK):
        out = mixed[:, span(k)] + part[0, :, span(k)] + sib_in2[0, :, span(k)].astype(f32)
        for cp in x2_copies[k]:
            cp.wait_recv()
        for d in (1, 2, 3):
            out = out + x_in2[d, :, span(k)].astype(f32)
        out_ref[:, span(k)] = out.astype(bf)

    for cp in everything:
        if not any(cp is done for done in reused):
            cp.wait_send()


def layer(
    queries, new_keys, new_values, cache_keys, cache_values, cache_len, residual_in,
    out_weight, norm_gain, router_weight, expert_ids, gate_proj, up_proj, down_proj,
):
    hbm = pl.BlockSpec(memory_space=pl.ANY)
    vmem = pl.BlockSpec(memory_space=pltpu.VMEM)
    bf, f32 = jnp.bfloat16, jnp.float32
    dma = pltpu.SemaphoreType.DMA
    total = NSEQ * (CDEV + TOK)
    plane = pltpu.VMEM((4, 4, SLOTS, WIDTH), bf)
    small = pltpu.VMEM((4, 4, 8, 128), f32)
    row = pltpu.VMEM((4, TOK, WIDTH), bf)
    out = pl.pallas_call(
        layer_kernel,
        out_shape=jax.ShapeDtypeStruct((TOK, WIDTH), bf),
        in_specs=[pl.BlockSpec(memory_space=pltpu.SMEM), vmem, vmem] + [hbm] * 11,
        out_specs=vmem,
        scratch_shapes=[
            pltpu.VMEM((DOCTOK, 512), bf),
            pltpu.VMEM((4, DOCTOK, 256), bf),
            pltpu.VMEM((total, 256), bf),
            pltpu.VMEM((total, 256), bf),
            pltpu.VMEM((4, DOCTOK, 256), f32),
            pltpu.VMEM((4, DOCTOK, HD), f32),
            pltpu.VMEM((2, 4, TOK, 512), bf),
            pltpu.VMEM((512, WIDTH), bf),
            pltpu.VMEM((TOK, WIDTH), bf),
            pltpu.VMEM((WIDTH, EXPERTS), bf),
            pltpu.VMEM((4, TOK, WIDTH), f32),
            row, row, row, row, row, row,
            pltpu.VMEM((TOK, WIDTH), f32),
            pltpu.VMEM((DOCTOK, WIDTH), bf),
            pltpu.VMEM((DOCTOK, EXPERTS), bf),
            pltpu.VMEM((DOCTOK, 2 * EXPERTS), f32),
            pltpu.VMEM((ROWS, DOCTOK), bf),
            pltpu.VMEM((DOCTOK, ROWS), bf),
            plane, plane, plane, plane, plane,
            small, small, small,
            pltpu.VMEM((WIDTH, FF), bf),
            pltpu.VMEM((WIDTH, FF), bf),
            pltpu.VMEM((FF, WIDTH), bf),
            pltpu.VMEM((ROWS, FF), f32),
            pltpu.VMEM((ROWS, FF), f32),
            pltpu.VMEM((ROWS, FF), bf),
            dma((11,)), dma((8,)), dma((8,)), dma((8,)), dma((8,)), dma((8, 2)), dma((8, 2)),
            dma((4, 2)), dma((4, 2)), dma((4, 2)), dma((4, 2)),
            dma((NCHUNK,)), dma((NCHUNK,)), dma((NCHUNK, 4)), dma((NCHUNK, 4)),
            dma((NCHUNK, 4)), dma((NCHUNK, 4)), dma((NCHUNK, 4)), dma((NCHUNK, 4)),
            dma((8,)), dma((8,)),
            dma((16 * NCHUNK + 8,)), dma((16 * NCHUNK + 8,)), dma((16 * NCHUNK,)), dma((16 * NCHUNK,)),
            dma((NCHUNK,)), dma((NCHUNK,)), dma((NCHUNK, 4)), dma((NCHUNK, 4)),
        ],
        compiler_params=pltpu.CompilerParams(
            collective_id=0, has_side_effects=True, vmem_limit_bytes=67043328
        ),
        name="whole_layer",
    )(cache_len, expert_ids[0], norm_gain.reshape(1, WIDTH), queries[0], new_keys[0],
      new_values[0], cache_keys[0], cache_values[0], out_weight, residual_in[0],
      router_weight, gate_proj[0], up_proj[0], down_proj[0])
    return out.reshape(1, TOK, WIDTH)


def solution(mesh):
    in_specs = (
        P("exp", "seq", None),
        P("exp", "seq", None),
        P("exp", "seq", None),
        P("exp", "seq", None),
        P("exp", "seq", None),
        P("exp"),
        P("exp", "seq", None),
        P("seq", None),
        P(),
        P(),
        P("exp", "seq", None),
        P(("seq", "exp"), None, None),
        P(("seq", "exp"), None, None),
        P(("seq", "exp"), None, None),
    )
    out_specs = P("exp", "seq", None)
    return jax.shard_map(layer, mesh=mesh, in_specs=in_specs, out_specs=out_specs, check_vma=False)
```

```python
import jax
import jax.numpy as jnp
from jax import lax
from jax.experimental import pallas as pl
from jax.experimental.pallas import tpu as pltpu
from jax.sharding import PartitionSpec as P

QH = 32
KVH = 4
HD = 128
TOPK = 8
NSEQ = 8
TOK = 64
DOCTOK = 512
CDEV = 512
WIDTH = 2048
LOG2E = 1.4426950408889634
MESH = pl.DeviceIdType.MESH


EXPERTS = 128
FF = 768
PEERS = 16
SLOTS = 48
CAP = 6
ROWS = PEERS * SLOTS
NCHUNK = 4
CHUNK = WIDTH // NCHUNK
AHEAD = 6
NT = (((1,), (1,)), ((), ()))


def layer_kernel(
    len_ref, ids_ref, gain_ref, q_hbm, kn_hbm, vn_hbm, kc_hbm, vc_hbm, w_hbm, res_hbm,
    router_hbm, wg_hbm, wu_hbm, wd_hbm, out_ref,
    qbuf, qext, kbuf, vbuf, acc, mbuf, attn, wbuf, resbuf, router, part,
    sib_out, sib_in, x_out, x_in, sib_in2, x_in2,
    mixed, tokens, table, gtable, pick, give, outbox, relay_out, inbox, relay_back, back,
    rbox, rrelay, rin, wg, wu, wd, hg, hu, act,
    loc_sem, c_send, c_recv, q_send, q_recv, n_send, n_recv, kv_send, kv_recv, fw_send, fw_recv,
    s_send, s_recv, x_send, x_recv, a_send, a_recv, f_send, f_recv, g_send, g_recv,
    d_send, d_recv, r_send, r_recv, s2_send, s2_recv, x2_send, x2_recv,
):
    me = lax.axis_index("seq")
    ex = lax.axis_index("exp")
    x, c = me // 2, lax.rem(me, 2)
    y, z = ex // 4, lax.rem(ex, 4)
    other = 1 - c
    sibling = (2 * x + other, ex)
    f32, bf = jnp.float32, jnp.bfloat16
    everything = []

    def chip(d):
        return lax.rem(x + d, 4)

    def along_x(d):
        return (2 * chip(d) + c, ex)

    def along_y(d):
        return (me, lax.rem(y + d, 4) * 4 + z)

    def along_z(d):
        return (me, y * 4 + lax.rem(z + d, 4))

    def in_row(d):
        return (lax.rem(me + d, NSEQ), ex)

    def block(s):
        return pl.ds(pl.multiple_of(s * TOK, TOK), TOK)

    def cached(s):
        return pl.ds(pl.multiple_of(s * CDEV, CDEV), CDEV)

    def fresh(s):
        return pl.ds(pl.multiple_of(NSEQ * CDEV + s * TOK, TOK), TOK)

    def head(h):
        return pl.ds(pl.multiple_of(h * HD, HD), HD)

    def span(k):
        return pl.ds(k * CHUNK, CHUNK)

    def send(src, dst, sends, recvs, to):
        cp = pltpu.make_async_remote_copy(
            src_ref=src, dst_ref=dst, send_sem=sends, recv_sem=recvs,
            device_id=to, device_id_type=MESH,
        )
        cp.start()
        everything.append(cp)
        return cp

    def fetch(i, src, dst):
        cp = pltpu.make_async_copy(src, dst, loc_sem.at[i])
        cp.start()
        return cp

    barrier = pltpu.get_barrier_semaphore()
    for d in range(1, NSEQ):
        pl.semaphore_signal(barrier, inc=1, device_id=in_row(d), device_id_type=MESH)
    for d in range(1, 4):
        pl.semaphore_signal(barrier, inc=1, device_id=along_y(d), device_id_type=MESH)
        pl.semaphore_signal(barrier, inc=1, device_id=along_z(d), device_id_type=MESH)

    lanes = pl.ds(0, HD)
    own_q = fetch(0, q_hbm.at[:, pl.ds(pl.multiple_of(me * 512, 512), 512)], qbuf.at[block(me), :])
    own_kn = fetch(1, kn_hbm.at[:, head(x)], kbuf.at[fresh(me), lanes])
    own_vn = fetch(2, vn_hbm.at[:, head(x)], vbuf.at[fresh(me), lanes])
    own_k = fetch(3, kc_hbm.at[:, head(x)], kbuf.at[cached(me), lanes])
    own_v = fetch(4, vc_hbm.at[:, head(x)], vbuf.at[cached(me), lanes])

    by_expert = jnp.zeros((EXPERTS, TOK), f32)
    expert = lax.broadcasted_iota(jnp.int32, (EXPERTS, TOK), 0)
    for k in range(TOPK):
        by_expert = by_expert + jnp.where(ids_ref[k:k + 1, :] == expert, f32(1.0), f32(0.0))
    same = (lax.broadcasted_iota(jnp.int32, (TOK, TOK), 1)
            == lax.broadcasted_iota(jnp.int32, (TOK, TOK), 0)).astype(f32)
    chosen = lax.dot_general(
        same.astype(bf), by_expert.astype(bf), NT, preferred_element_type=f32
    )
    before = (lax.broadcasted_iota(jnp.int32, (TOK, TOK), 1)
              < lax.broadcasted_iota(jnp.int32, (TOK, TOK), 0)).astype(f32)
    rank = jnp.dot(before.astype(bf), chosen.astype(bf), preferred_element_type=f32)
    first = (CAP * me + 1).astype(f32)
    table[block(me), :] = jnp.where(chosen > 0, rank + first, f32(0.0)).astype(bf)

    pl.semaphore_wait(barrier, NSEQ - 1 + 6)
    q_copies, n_copies, c_copies = [], [], []
    for d in (4, 2, 6, 3, 5, 1, 7):
        to = lax.rem(me + d, NSEQ)
        q_copies.append(send(
            q_hbm.at[:, pl.ds(pl.multiple_of(to * 512, 512), 512)], qbuf.at[block(me), :],
            q_send.at[d], q_recv.at[d], in_row(d)))
    for d in (4, 2, 6, 3, 5, 1, 7):
        h = lax.rem(me + d, NSEQ) // 2
        for i, (src, dst) in enumerate(((kn_hbm, kbuf), (vn_hbm, vbuf))):
            n_copies.append(send(
                src.at[:, head(h)], dst.at[fresh(me), lanes],
                n_send.at[d, i], n_recv.at[d, i], in_row(d)))
    fw_copies = {0: [
        send(src.at[:, head(x)], dst.at[cached(me), lanes],
             fw_send.at[0, i], fw_recv.at[0, i], sibling)
        for i, (src, dst) in enumerate(((kc_hbm, kbuf), (vc_hbm, vbuf)))
    ]}
    kv_copies = {}
    for d in (1, 3, 2):
        kv_copies[d] = [
            send(src.at[:, head(chip(d))], dst.at[cached(me), lanes],
                 kv_send.at[d, i], kv_recv.at[d, i], along_x(d))
            for i, (src, dst) in enumerate(((kc_hbm, kbuf), (vc_hbm, vbuf)))
        ]
    for d in range(1, NSEQ):
        view = table.at[block(me), :]
        c_copies.append(send(view, view, c_send.at[d], c_recv.at[d], in_row(d)))
    get_w = fetch(5, w_hbm, wbuf)
    get_res = fetch(6, res_hbm, resbuf)
    get_router = fetch(7, router_hbm, router)
    get_wg = fetch(8, wg_hbm, wg)
    get_wu = fetch(9, wu_hbm, wu)
    get_wd = fetch(10, wd_hbm, wd)

    total = NSEQ * (CDEV + TOK)
    lane = lax.broadcasted_iota(jnp.int32, (total, HD), 1)
    pos = lax.broadcasted_iota(jnp.int32, (total, HD), 0)
    hidden = (pos >= len_ref[0]) & (pos < NSEQ * CDEV) & (lane == 0)
    kbuf[:, HD:] = jnp.where(hidden, f32(-1e30), f32(0.0)).astype(bf)
    vbuf[:, HD:] = jnp.ones((total, HD), bf)
    acc[...] = jnp.zeros_like(acc)
    mbuf[...] = jnp.full(mbuf.shape, -3e38, f32)
    unit = (lax.broadcasted_iota(jnp.int32, (DOCTOK, HD), 1) == 0).astype(f32).astype(bf)
    for h in range(4):
        qext[h, :, HD:] = unit

    for cp in q_copies:
        cp.wait_recv()
    own_q.wait()
    for h in range(4):
        qext[h, :, :HD] = qbuf[:, h * HD:(h + 1) * HD]

    factor = f32(LOG2E / (HD ** 0.5))

    def attend(begin, count, causal):
        keys_at = pl.ds(begin, count)

        def heads_of(i, carry):
            tiles = [(i * 2 + j, r * 256) for j in range(2) for r in range(2)]
            scores = []
            for h, r in tiles:
                s = lax.dot_general(
                    qext[h, pl.ds(r, 256), :], kbuf[keys_at, :], NT, preferred_element_type=f32
                )
                if causal:
                    t = lax.broadcasted_iota(jnp.int32, s.shape, 0) + r
                    u = lax.broadcasted_iota(jnp.int32, s.shape, 1)
                    s = jnp.where(u <= t, s, f32(-1e30))
                scores.append(s)
            for (h, r), s in zip(tiles, scores):
                rows = pl.ds(r, 256)
                m_old = mbuf[h, rows, :]
                m_new = jnp.maximum(m_old, jnp.max(s, axis=1, keepdims=True))
                mbuf[h, rows, :] = m_new
                alpha = jnp.exp2((m_old - m_new) * factor)
                p = jnp.exp2((s - m_new[:, :1]) * factor).astype(bf)
                pv = jnp.dot(p, vbuf[keys_at, :], preferred_element_type=f32)
                acc[h, rows, :HD] = acc[h, rows, :HD] * alpha + pv[:, :HD]
                acc[h, rows, HD:] = acc[h, rows, HD:] * alpha + pv[:, HD:]
            return carry

        lax.fori_loop(0, 2, heads_of, 0)

    def forward_kv(d):
        for cp in kv_copies[d]:
            cp.wait_recv()
        src = 2 * lax.rem(x + 4 - d, 4) + c
        fw_copies[d] = [
            send(view, view, fw_send.at[d, i], fw_recv.at[d, i], sibling)
            for i, view in enumerate((kbuf.at[cached(src), lanes], vbuf.at[cached(src), lanes]))
        ]

    def attend_chip(d):
        for cp in fw_copies[d]:
            cp.wait_recv()
        attend(pl.multiple_of(lax.rem(x + 4 - d, 4) * 1024, 1024), 1024, False)

    own_k.wait()
    own_v.wait()
    attend_chip(0)
    own_kn.wait()
    own_vn.wait()
    for cp in n_copies:
        cp.wait_recv()
    attend(NSEQ * CDEV, DOCTOK, True)
    forward_kv(1)
    forward_kv(3)

    qi = lax.broadcasted_iota(jnp.int32, (ROWS, EXPERTS), 0)
    ei = (lax.broadcasted_iota(jnp.int32, (ROWS, EXPERTS), 1) - me * PEERS) * SLOTS
    owner = jnp.where((qi >= ei) & (qi < ei + SLOTS), f32(1.0), f32(0.0)).astype(bf)

    def within(shape, axis):
        at = lax.broadcasted_iota(jnp.int32, shape, axis)
        low = at + 1
        for e in range(1, PEERS):
            low = jnp.where(at >= e * SLOTS, at + 1 - e * SLOTS, low)
        return low.astype(f32)

    for cp in c_copies:
        cp.wait_recv()
    by_row = lax.dot_general(owner, table[...], NT, preferred_element_type=f32)
    pick[...] = jnp.where(by_row == within((ROWS, 128), 0)[:, :1], f32(1.0), f32(0.0)).astype(bf)

    attend_chip(1)
    forward_kv(2)
    attend_chip(3)
    attend_chip(2)

    get_w.wait()
    get_res.wait()
    get_router.wait()
    for d in range(4):
        for i, core in enumerate((other, c)):
            at = block(2 * chip(d) + core)
            for h in range(4):
                attn[i, d, :, h * HD:(h + 1) * HD] = (
                    acc[h, at, :HD] / acc[h, at, HD:]
                ).astype(bf)

    s_copies, x_copies = {}, {}

    def sum_cores(k):
        sib_out[:, :, span(k)] = jnp.dot(
            attn[0].reshape(4 * TOK, 512), wbuf[:, span(k)], preferred_element_type=f32
        ).astype(bf).reshape(4, TOK, CHUNK)
        view = sib_out.at[:, :, span(k)]
        s_copies[k] = send(view, sib_in.at[:, :, span(k)], s_send.at[k], s_recv.at[k], sibling)
        part[:, :, span(k)] = jnp.dot(
            attn[1].reshape(4 * TOK, 512), wbuf[:, span(k)], preferred_element_type=f32
        ).reshape(4, TOK, CHUNK)

    def sum_chips(k):
        s_copies[k].wait_recv()
        x_copies[k] = []
        for d in (2, 1, 3):
            x_out[d, :, span(k)] = (
                part[d, :, span(k)] + sib_in[d, :, span(k)].astype(f32)
            ).astype(bf)
            x_copies[k].append(send(
                x_out.at[d, :, span(k)], x_in.at[d, :, span(k)],
                x_send.at[k, d], x_recv.at[k, d], along_x(d)))

    a_copies, f_copies = {}, {}

    def spread(k):
        mine = (resbuf[:, span(k)].astype(f32) + part[0, :, span(k)]
                + sib_in[0, :, span(k)].astype(f32))
        for cp in x_copies[k]:
            cp.wait_recv()
        for d in (1, 2, 3):
            mine = mine + x_in[d, :, span(k)].astype(f32)
        mixed[:, span(k)] = mine
        tokens[block(me), span(k)] = (mine * gain_ref[:, span(k)]).astype(bf)
        view = tokens.at[block(me), span(k)]
        a_copies[k] = {
            d: send(view, view, a_send.at[k, d], a_recv.at[k, d],
                    sibling if d == 0 else along_x(d))
            for d in (2, 1, 3, 0)
        }

    def forward(k):
        f_copies[k] = []
        for d in (1, 3, 2):
            a_copies[k][d].wait_recv()
            view = tokens.at[block(2 * lax.rem(x + 4 - d, 4) + c), span(k)]
            f_copies[k].append(send(view, view, f_send.at[k, d], f_recv.at[k, d], sibling))

    def hop(even, at, source, target, sends, recvs, base):
        copies = []
        for d in (1, 3, 2):
            if even:
                src, dst, to = source.at[lax.rem(y + d, 4), :, :, at], target.at[y, :, :, at], along_y(d)
            else:
                src, dst, to = source.at[:, lax.rem(z + d, 4), :, at], target.at[:, z, :, at], along_z(d)
            copies.append(send(src, dst, sends.at[base + d], recvs.at[base + d], to))
        if even:
            target[y, :, :, at] = source[y, :, :, at]
        else:
            target[:, z, :, at] = source[:, z, :, at]
        return copies

    def both(k, turn, source, target, sends, recvs, base):
        copies = []
        for i in range(2):
            at = pl.ds(k * CHUNK + i * (CHUNK // 2), CHUNK // 2)
            copies += hop((i + turn) % 2 == 0, at, source, target, sends, recvs, base + 4 * i)
        return copies

    d_first, d_second, r_first, r_second = {}, {}, {}, {}

    def dispatch(k):
        a_copies[k][0].wait_recv()
        for cp in f_copies[k]:
            cp.wait_recv()
        outbox[:, :, :, span(k)] = jnp.dot(
            pick[...], tokens[:, span(k)], preferred_element_type=f32
        ).astype(bf).reshape(4, 4, SLOTS, CHUNK)
        d_first[k] = both(k, 0, outbox, relay_out, d_send, d_recv, 16 * k)

    def dispatch_on(k):
        for cp in d_first[k]:
            cp.wait_recv()
        d_second[k] = both(k, 1, relay_out, inbox, d_send, d_recv, 16 * k + 8)

    stages = (sum_cores, sum_chips, spread, forward, dispatch)
    for t in range(NCHUNK + len(stages) - 1):
        for i, stage in enumerate(stages):
            if 0 <= t - i < NCHUNK:
                stage(t - i)
        if t == NCHUNK + 1:
            mx = mixed[...]
            factor_of = f32(1.0) / jnp.sqrt(jnp.mean(mx * mx, axis=1, keepdims=True) + 1e-06)
            normed = (mx * factor_of * gain_ref[...]).astype(bf)
            logits = jnp.dot(normed, router[...], preferred_element_type=f32)
            expo = jnp.where(chosen > 0, jnp.exp(logits), f32(0.0))
            gtable[block(me), :EXPERTS] = expo / jnp.sum(expo, axis=1, keepdims=True)
            gtable[block(me), EXPERTS:] = jnp.broadcast_to(factor_of, (TOK, EXPERTS))
            view = gtable.at[block(me), :]
            g_copies = [
                send(view, view, g_send.at[d], g_recv.at[d], in_row(d)) for d in range(1, NSEQ)
            ]
        if t >= AHEAD:
            dispatch_on(t - AHEAD)

    for cp in g_copies:
        cp.wait_recv()
    fac = gtable[:, EXPERTS:]
    high = fac.astype(bf)
    rest = fac - high.astype(f32)
    mid = rest.astype(bf)
    low = (rest - mid.astype(f32)).astype(bf)
    by_slot = (jnp.dot(pick[...], high, preferred_element_type=f32)
               + jnp.dot(pick[...], mid, preferred_element_type=f32)
               + jnp.dot(pick[...], low, preferred_element_type=f32))
    slot_lane = lax.broadcasted_iota(jnp.int32, (PEERS, SLOTS, 128), 2)
    slot_row = lax.broadcasted_iota(jnp.int32, (PEERS, SLOTS, 128), 1)
    lined = jnp.sum(
        jnp.where(slot_lane == slot_row, by_slot.reshape(PEERS, SLOTS, 128), f32(0.0)), axis=1
    )
    rbox[...] = jnp.broadcast_to(lined[:, None, :], (PEERS, 8, 128)).reshape(4, 4, 8, 128)
    every = pl.ds(0, 128)
    rf = hop(True, every, rbox, rrelay, d_send, d_recv, 16 * NCHUNK)

    for k in range(NCHUNK + 4 - AHEAD, NCHUNK):
        dispatch_on(k)
    for cp in rf:
        cp.wait_recv()
    rs = hop(False, every, rrelay, rin, d_send, d_recv, 16 * NCHUNK + 4)

    by_token = lax.dot_general(table[...], owner, NT, preferred_element_type=f32)
    share = lax.dot_general(gtable[:, :EXPERTS].astype(bf), owner, NT, preferred_element_type=f32)
    give[...] = jnp.where(by_token == within((8, ROWS), 1)[:1, :], share, f32(0.0)).astype(bf)

    get_wg.wait()
    get_wu.wait()
    for k in range(NCHUNK):
        for cp in d_second[k]:
            cp.wait_recv()
        rows = inbox[:, :, :, span(k)].reshape(ROWS, CHUNK)
        g = jnp.dot(rows, wg[span(k), :], preferred_element_type=f32)
        u = jnp.dot(rows, wu[span(k), :], preferred_element_type=f32)
        if k == 0:
            hg[...] = g
            hu[...] = u
        else:
            hg[...] += g
            hu[...] += u
    for cp in rs:
        cp.wait_recv()
    got = rin[...].reshape(PEERS, 8, 128)[:, :1, :]
    scale = jnp.sum(jnp.where(slot_lane == slot_row, got, f32(0.0)), axis=2, keepdims=True)
    scale = scale.reshape(ROWS, 1)
    g = hg[...] * scale
    act[...] = (g / (f32(1.0) + jnp.exp(-g)) * (hu[...] * scale)).astype(bf)
    get_wd.wait()
    reused = [cp for k in range(NCHUNK) for cp in d_first[k] + x_copies[k] + [s_copies[k]]]
    for cp in reused:
        cp.wait_send()
    for k in range(NCHUNK):
        outbox[:, :, :, span(k)] = jnp.dot(
            act[...], wd[:, span(k)], preferred_element_type=f32
        ).astype(bf).reshape(4, 4, SLOTS, CHUNK)
        r_first[k] = both(k, 0, outbox, relay_back, r_send, r_recv, 16 * k)

    for k in range(NCHUNK):
        for cp in r_first[k]:
            cp.wait_recv()
        r_second[k] = both(k, 1, relay_back, back, r_send, r_recv, 16 * k + 8)

    s2_copies, x2_copies = {}, {}

    def combine(k):
        for cp in r_second[k]:
            cp.wait_recv()
        returned = back[:, :, :, span(k)].reshape(ROWS, CHUNK)
        for d in (2, 1, 3, 0):
            sib_out[d, :, span(k)] = jnp.dot(
                give[block(2 * chip(d) + other), :], returned, preferred_element_type=f32
            ).astype(bf)
        view = sib_out.at[:, :, span(k)]
        s2_copies[k] = send(view, sib_in2.at[:, :, span(k)], s2_send.at[k], s2_recv.at[k], sibling)
        for d in (2, 1, 3, 0):
            part[d, :, span(k)] = jnp.dot(
                give[block(2 * chip(d) + c), :], returned, preferred_element_type=f32
            )

    def combine_chips(k):
        s2_copies[k].wait_recv()
        x2_copies[k] = []
        for d in (2, 1, 3):
            x_out[d, :, span(k)] = (
                part[d, :, span(k)] + sib_in2[d, :, span(k)].astype(f32)
            ).astype(bf)
            x2_copies[k].append(send(
                x_out.at[d, :, span(k)], x_in2.at[d, :, span(k)],
                x2_send.at[k, d], x2_recv.at[k, d], along_x(d)))

    for k in range(NCHUNK):
        combine(k)
        if k:
            combine_chips(k - 1)
    combine_chips(NCHUNK - 1)
    for k in range(NCHUNK):
        out = mixed[:, span(k)] + part[0, :, span(k)] + sib_in2[0, :, span(k)].astype(f32)
        for cp in x2_copies[k]:
            cp.wait_recv()
        for d in (1, 2, 3):
            out = out + x_in2[d, :, span(k)].astype(f32)
        out_ref[:, span(k)] = out.astype(bf)

    for cp in everything:
        if not any(cp is done for done in reused):
            cp.wait_send()


def layer(
    queries, new_keys, new_values, cache_keys, cache_values, cache_len, residual_in,
    out_weight, norm_gain, router_weight, expert_ids, gate_proj, up_proj, down_proj,
):
    hbm = pl.BlockSpec(memory_space=pl.ANY)
    vmem = pl.BlockSpec(memory_space=pltpu.VMEM)
    bf, f32 = jnp.bfloat16, jnp.float32
    dma = pltpu.SemaphoreType.DMA
    total = NSEQ * (CDEV + TOK)
    plane = pltpu.VMEM((4, 4, SLOTS, WIDTH), bf)
    small = pltpu.VMEM((4, 4, 8, 128), f32)
    row = pltpu.VMEM((4, TOK, WIDTH), bf)
    out = pl.pallas_call(
        layer_kernel,
        out_shape=jax.ShapeDtypeStruct((TOK, WIDTH), bf),
        in_specs=[pl.BlockSpec(memory_space=pltpu.SMEM), vmem, vmem] + [hbm] * 11,
        out_specs=vmem,
        scratch_shapes=[
            pltpu.VMEM((DOCTOK, 512), bf),
            pltpu.VMEM((4, DOCTOK, 256), bf),
            pltpu.VMEM((total, 256), bf),
            pltpu.VMEM((total, 256), bf),
            pltpu.VMEM((4, DOCTOK, 256), f32),
            pltpu.VMEM((4, DOCTOK, HD), f32),
            pltpu.VMEM((2, 4, TOK, 512), bf),
            pltpu.VMEM((512, WIDTH), bf),
            pltpu.VMEM((TOK, WIDTH), bf),
            pltpu.VMEM((WIDTH, EXPERTS), bf),
            pltpu.VMEM((4, TOK, WIDTH), f32),
            row, row, row, row, row, row,
            pltpu.VMEM((TOK, WIDTH), f32),
            pltpu.VMEM((DOCTOK, WIDTH), bf),
            pltpu.VMEM((DOCTOK, EXPERTS), bf),
            pltpu.VMEM((DOCTOK, 2 * EXPERTS), f32),
            pltpu.VMEM((ROWS, DOCTOK), bf),
            pltpu.VMEM((DOCTOK, ROWS), bf),
            plane, plane, plane, plane, plane,
            small, small, small,
            pltpu.VMEM((WIDTH, FF), bf),
            pltpu.VMEM((WIDTH, FF), bf),
            pltpu.VMEM((FF, WIDTH), bf),
            pltpu.VMEM((ROWS, FF), f32),
            pltpu.VMEM((ROWS, FF), f32),
            pltpu.VMEM((ROWS, FF), bf),
            dma((11,)), dma((8,)), dma((8,)), dma((8,)), dma((8,)), dma((8, 2)), dma((8, 2)),
            dma((4, 2)), dma((4, 2)), dma((4, 2)), dma((4, 2)),
            dma((NCHUNK,)), dma((NCHUNK,)), dma((NCHUNK, 4)), dma((NCHUNK, 4)),
            dma((NCHUNK, 4)), dma((NCHUNK, 4)), dma((NCHUNK, 4)), dma((NCHUNK, 4)),
            dma((8,)), dma((8,)),
            dma((16 * NCHUNK + 8,)), dma((16 * NCHUNK + 8,)), dma((16 * NCHUNK,)), dma((16 * NCHUNK,)),
            dma((NCHUNK,)), dma((NCHUNK,)), dma((NCHUNK, 4)), dma((NCHUNK, 4)),
        ],
        compiler_params=pltpu.CompilerParams(
            collective_id=0, has_side_effects=True, vmem_limit_bytes=67043328
        ),
        name="whole_layer",
    )(cache_len, expert_ids[0].T, norm_gain.reshape(1, WIDTH), queries[0], new_keys[0],
      new_values[0], cache_keys[0], cache_values[0], out_weight, residual_in[0],
      router_weight, gate_proj[0], up_proj[0], down_proj[0])
    return out.reshape(1, TOK, WIDTH)


def solution(mesh):
    in_specs = (
        P("exp", "seq", None),
        P("exp", "seq", None),
        P("exp", "seq", None),
        P("exp", "seq", None),
        P("exp", "seq", None),
        P("exp"),
        P("exp", "seq", None),
        P("seq", None),
        P(),
        P(),
        P("exp", "seq", None),
        P(("seq", "exp"), None, None),
        P(("seq", "exp"), None, None),
        P(("seq", "exp"), None, None),
    )
    out_specs = P("exp", "seq", None)
    return jax.shard_map(layer, mesh=mesh, in_specs=in_specs, out_specs=out_specs, check_vma=False)
```
